128 devices in a mesh: dp: 64 (over y_lo, x, z, core), mp: 2 (over y_hi).
Axes of the slice: x: 4, y: 4 (y_hi: 2, y_lo: 2; y = y_hi * 2 + y_lo), z: 4, core: 2. Of those that a mesh axis runs over, the one named last changes fastest.
Arguments:
- img_feat: bfloat16 [49152, 1152], P('dp'), may hold values from -16 to 16
- txt_feat: bfloat16 [49152, 1152], P('dp'), may hold values from -16 to 16
- img_head: bfloat16 [1152, 1152], P('dp', 'mp'), may hold values from -0.1875 to 0.1875
- txt_head: bfloat16 [1152, 1152], P('dp', 'mp'), may hold values from -0.1875 to 0.1875
- logit_scale: float32 [1], replicated, may hold values from 4 to 16
- logit_bias: float32 [1], replicated, may hold values from -6 to -2
Outputs:
- img_head_grad: float32 [1152, 1152], P('dp', 'mp')
- txt_head_grad: float32 [1152, 1152], P('dp', 'mp')
The draws below stay inside these ranges and needn't reach their ends.
All inputs are finite; a program needn't handle non-finite values.
Results may differ from the reference program's by a relative error of at most 0.0019.
Values may be sent and summed in bfloat16 or wider, within the bound.
No kernel may reach another device: no remote copies, remote signals or barrier semaphores. Data moves between devices by JAX's collectives and lax.ppermute only.
A program may use at most 64 MiB of HBM per device.

```python
import math
import jax
import jax.numpy as jnp
from jax import lax

D = 1152
E = 1152
BLOCK = 768
SHIFTS = 4
PAIRS = 49152
N_DP = 64


def strengthened(drawn, rng, source, target, blocks, factor):
    def block_of(position):
        return (jnp.arange(drawn.shape[position]) // (drawn.shape[position] // blocks)).reshape((-1,) + (1,) * (drawn.ndim - 1 - position))

    one_side = jax.random.permutation(rng, blocks)[block_of(target)]
    other_side = (block_of(target) + blocks // 2) % blocks
    return jnp.where((block_of(source) == one_side) | (block_of(source) == other_side), factor * drawn, drawn)


def steps_of(key, extent, cuts, smallest, high):
    def one(position, blocks):
        steps = jax.random.uniform(jax.random.fold_in(jax.random.fold_in(key, 6), position), (blocks,), jnp.float32, smallest / len(cuts), high / len(cuts))
        return jnp.repeat(jnp.exp(steps), extent[position] // blocks).reshape((-1,) + (1,) * (len(extent) - position - 1))

    gain = one(*cuts[0])
    for cut in cuts[1:]:
        gain = gain * one(*cut)
    return gain


def normal_values(own_key, shape, width, most, split=(), kind=jnp.bfloat16):
    level = steps_of(own_key, shape, split, -0.22, 0.18) if split else 1.0
    entries = jax.random.normal(own_key, shape, jnp.float32) * width * level
    return jnp.minimum(jnp.maximum(entries, -most), most).astype(kind)


def heavy_noise(stream_key, dims, deviation, most, split, heavy, kind=jnp.bfloat16):
    values = deviation * jax.random.normal(stream_key, dims, jnp.float32)
    if split:
        values = values * steps_of(stream_key, dims, split, -0.22, 0.18)
    return jnp.clip(strengthened(values, jax.random.fold_in(stream_key, 3), *heavy), -most, most).astype(kind)


def setup_inputs(seed: int = 0) -> dict:
    seeds = jax.random.split(jax.random.key(seed), 7)
    img_feat = heavy_noise(seeds[0], (PAIRS, D), 1.0, 16.0, ((0, 64),), (0, 1, 64, 4.0))
    txt_feat = heavy_noise(seeds[1], (PAIRS, D), 1.0, 16.0, ((0, 64),), (0, 1, 64, 4.0))
    img_head = normal_values(seeds[2], (D, E), D ** -0.5, 0.1875, ((0, 64), (1, 2)))
    txt_head = normal_values(seeds[3], (D, E), D ** -0.5, 0.1875, ((0, 64), (1, 2)))
    logit_scale = jnp.clip(jnp.exp(jax.random.uniform(seeds[4], (1,), jnp.float32, math.log(4.0), math.log(16.0))), 4.0, 16.0)
    logit_bias = jnp.clip(jax.random.uniform(seeds[5], (1,), jnp.float32, -6.0, -2.0), -6.0, -2.0)
    return {"img_feat": img_feat, "txt_feat": txt_feat, "img_head": img_head, "txt_head": txt_head, "logit_scale": logit_scale, "logit_bias": logit_bias}


epsilon = 1e-06

def pair_weights(logits, own):
    label = 2.0 * own - 1.0
    return -label * jax.nn.sigmoid(-label * logits)

def rounded(values):
    low = lax.optimization_barrier(values.astype(jnp.bfloat16))
    return low.astype(jnp.float32)

def reference(img_feat, txt_feat, img_head, txt_head, logit_scale, logit_bias):
    img_proj = jnp.dot(img_feat, img_head, preferred_element_type=jnp.float32)
    txt_proj = jnp.dot(txt_feat, txt_head, preferred_element_type=jnp.float32)
    img_len = jnp.sqrt(lax.optimization_barrier(jnp.sum(img_proj * img_proj, axis=1, keepdims=True)) + epsilon)
    txt_len = jnp.sqrt(lax.optimization_barrier(jnp.sum(txt_proj * txt_proj, axis=1, keepdims=True)) + epsilon)
    img_unit = img_proj / img_len
    txt_unit = txt_proj / txt_len
    img_low = rounded(img_unit).reshape(N_DP, BLOCK, E)
    txt_low = rounded(txt_unit).reshape(N_DP, BLOCK, E)
    scale_value = logit_scale[0]
    bias_value = logit_bias[0]
    own = jnp.eye(BLOCK, dtype=jnp.float32)
    img_acc = jnp.zeros((N_DP, BLOCK, E), jnp.float32)
    txt_acc = jnp.zeros((N_DP, BLOCK, E), jnp.float32)
    for offset in range(SHIFTS):
        visitor = jnp.roll(txt_low, offset, axis=0)
        dots = jnp.einsum('kae,kce->kac', img_low, visitor)
        logits = scale_value * dots + bias_value
        mask = own if offset == 0 else jnp.zeros_like(own)
        weights = rounded(pair_weights(logits, mask))
        img_acc = img_acc + scale_value * jnp.einsum('kac,kce->kae', weights, visitor)
        moved = scale_value * jnp.einsum('kac,kae->kce', weights, img_low)
        txt_acc = txt_acc + jnp.roll(moved, -offset, axis=0)
    img_unit_grad = img_acc.reshape(N_DP * BLOCK, E)
    txt_unit_grad = txt_acc.reshape(N_DP * BLOCK, E)
    img_inner = lax.optimization_barrier(jnp.sum(img_unit * img_unit_grad, axis=1, keepdims=True))
    txt_inner = lax.optimization_barrier(jnp.sum(txt_unit * txt_unit_grad, axis=1, keepdims=True))
    img_pre = ((img_unit_grad - img_unit * img_inner) / img_len).astype(jnp.bfloat16)
    txt_pre = ((txt_unit_grad - txt_unit * txt_inner) / txt_len).astype(jnp.bfloat16)
    img_head_grad = jnp.dot(img_feat.T, img_pre, preferred_element_type=jnp.float32)
    txt_head_grad = jnp.dot(txt_feat.T, txt_pre, preferred_element_type=jnp.float32)
    return (img_head_grad, txt_head_grad)
```

```python
import jax
import jax.numpy as jnp
from jax import lax
from jax.experimental import pallas as pl
from jax.experimental.pallas import tpu as pltpu
from jax.sharding import Mesh
from jax.sharding import PartitionSpec as P

SHIFTS = 4
DP = ("yl", "x", "z", "c")
AXES = ("yl", "x", "z", "c", "yh")
SIZES = (2, 4, 4, 2, 2)
RING = 4
WIDE = 512

epsilon = 1e-06
f32 = jnp.float32
bf16 = jnp.bfloat16


def place(yl, x, z, c, yh):
    at = 0
    for coordinate, size in zip((yl, x, z, c, yh), SIZES):
        at = at * size + coordinate
    return at


def moved(array, target):
    pairs = []
    for yl in range(2):
        for x in range(4):
            for z in range(4):
                for c in range(2):
                    for yh in range(2):
                        pairs.append((place(yl, x, z, c, yh), place(*target(yl, x, z, c, yh))))
    return lax.ppermute(array, AXES, pairs)


def along_x(d):
    return lambda yl, x, z, c, yh: (yl, (x + d) % 4, z, c, yh)


def along_y(d):
    def to(yl, x, z, c, yh):
        y = (yh * 2 + yl + d) % 4
        return (y % 2, x, z, c, y // 2)

    return to


def along_z(d):
    return lambda yl, x, z, c, yh: (yl, x, (z + d) % 4, c, yh)


def partner(yl, x, z, c, yh):
    return (yl, x, z, 1 - c, yh)


def by_core(zero, one):
    return lambda yl, x, z, c, yh: (one if c else zero)(yl, x, z, c, yh)


def next_block(yl, x, z, c, yh):
    k = (((yl * 4 + x) * 4 + z) * 2 + c + 1) % 64
    return (k // 32, k // 8 % 4, k // 2 % 4, k % 2, yh)


def tdot(left, right):
    return lax.dot_general(left, right, (((0,), (0,)), ((), ())), preferred_element_type=f32)


def rdot(left, right):
    return lax.dot_general(left, right, (((1,), (1,)), ((), ())), preferred_element_type=f32)


def position(role, x, y, near, far):
    px = jnp.where(role == 0, (x + near) % 4, (x + far) % 4)
    py = jnp.where(role == 0, (y + far) % 4, (y + near) % 4)
    return px, py


def assemble_kernel(at, *refs):
    pieces, whole = refs[:8], refs[8]
    c, x, y = at[0], at[1], at[2]
    for source in range(2):
        role = c if source == 0 else 1 - c
        for far in range(RING):
            for near in range(RING):
                px, py = position(role, x, y, near, far)
                rows = pl.ds(pl.multiple_of((py % 2 * 4 + px) * 144, 144), 144)
                piece = pieces[source * 4 + far].at[near]
                for half in range(2):

                    @pl.when(py // 2 == half)
                    def _():
                        whole[role, rows, half * WIDE : (half + 1) * WIDE] = piece[:, :WIDE]
                        tail = 2 * WIDE + half * 64
                        whole[role, rows, tail : tail + 64] = piece[:, WIDE:]


def assemble(at, pieces):
    return pl.pallas_call(
        assemble_kernel,
        out_shape=jax.ShapeDtypeStruct((2, 1152, 1152), bf16),
        in_specs=[pl.BlockSpec(memory_space=pltpu.SMEM)]
        + [pl.BlockSpec(memory_space=pltpu.VMEM)] * 8,
        out_specs=pl.BlockSpec(memory_space=pltpu.VMEM),
        name="assemble",
    )(at, *pieces)


def pack_kernel(at, kept, come, *outs):
    c, x, y = at[0], at[1], at[2]
    for near in range(RING):
        for far in range(RING):
            py = jnp.where(c == 0, (y + near) % 4, (y + far) % 4)
            px = jnp.where(c == 0, (x + far) % 4, (x + near) % 4)
            rows = pl.ds(pl.multiple_of((py % 2 * 4 + px) * 144, 144), 144)
            for half in range(2):

                @pl.when(py // 2 == half)
                def _():
                    out = outs[near].at[far]
                    wide = slice(half * WIDE, (half + 1) * WIDE)
                    tail = slice(2 * WIDE + half * 64, 2 * WIDE + half * 64 + 64)
                    out[:, :WIDE] = (kept[rows, wide] + come[rows, wide]).astype(out.dtype)
                    out[:, WIDE:] = (kept[rows, tail] + come[rows, tail]).astype(out.dtype)


def pack(at, kept, come):
    shape = (RING, 144, 576)
    return pl.pallas_call(
        pack_kernel,
        out_shape=[jax.ShapeDtypeStruct(shape, f32)] * 4,
        in_specs=[pl.BlockSpec(memory_space=pltpu.SMEM)]
        + [pl.BlockSpec(memory_space=pltpu.VMEM)] * 2,
        out_specs=[pl.BlockSpec(memory_space=pltpu.VMEM)] * 4,
        name="pack",
    )(at, kept, come)


def rolled(parts, index, rows):
    twice = jnp.concatenate(parts + parts, axis=0)
    return lax.dynamic_slice_in_dim(twice, (RING - index) % RING * rows, RING * rows, 0)


def per_device(img_feat, txt_feat, img_head, txt_head, logit_scale, logit_bias):
    yl, x, z, c, yh = (lax.axis_index(a) for a in AXES)
    y = yh * 2 + yl
    at = jnp.stack([c, x, y]).astype(jnp.int32)

    half_rows = txt_feat.shape[0] // 2
    row_base = yh * half_rows
    visitors = [lax.dynamic_slice_in_dim(txt_feat, row_base, half_rows, 0)]
    for _ in range(1, SHIFTS):
        visitors.append(moved(visitors[-1], next_block))

    first = c == 0
    mine = jnp.where(first, img_head, txt_head)
    come = moved(jnp.where(first, txt_head, img_head), partner)
    rows36 = jnp.where(
        first, jnp.concatenate([mine, come], 0), jnp.concatenate([come, mine], 0)
    )
    parts = [rows36] + [moved(rows36, along_z(-d)) for d in range(1, RING)]
    piece = rolled(parts, z, 36)
    near = [piece] + [moved(piece, by_core(along_x(-d), along_y(-d))) for d in range(1, RING)]
    near = jnp.stack(near)
    far = [near] + [moved(near, by_core(along_y(-d), along_x(-d))) for d in range(1, RING)]
    other = [moved(a, partner) for a in far]
    heads = assemble(at, far + other)

    def units(feat, head):
        proj = jnp.dot(feat, head, preferred_element_type=f32)
        length = jnp.sqrt(jnp.sum(proj * proj, axis=1) + epsilon)[:, None]
        return proj / length, length

    img_unit, img_len = units(img_feat, heads[0])
    txt_rows = jnp.concatenate(visitors, axis=0)
    txt_unit, txt_len = units(txt_rows, heads[1])
    img_low = img_unit.astype(bf16)
    txt_low = txt_unit.astype(bf16)
    scale_value = logit_scale[0]
    bias_value = logit_bias[0]
    logits = scale_value * rdot(img_low, txt_low) + bias_value
    rows = lax.broadcasted_iota(jnp.int32, logits.shape, 0)
    cols = lax.broadcasted_iota(jnp.int32, logits.shape, 1)
    label = jnp.where((rows == row_base + cols) & (cols < half_rows), 1.0, -1.0)
    weights = (-label * jax.nn.sigmoid(-label * logits)).astype(bf16)
    img_grad = scale_value * jnp.dot(weights, txt_low, preferred_element_type=f32)
    txt_grad = scale_value * tdot(weights, img_low)

    def before(unit, length, grad):
        inner = jnp.sum(unit * grad, axis=1)[:, None]
        return ((grad - unit * inner) / length).astype(bf16)

    img_part = tdot(img_feat, before(img_unit, img_len, img_grad))
    txt_part = tdot(txt_rows, before(txt_unit, txt_len, txt_grad))

    kept = jnp.where(first, img_part, txt_part)
    come = moved(jnp.where(first, txt_part, img_part), partner)
    packed = pack(at, kept, come)
    total = packed[0]
    for d in range(1, RING):
        total = total + moved(packed[d], by_core(along_y(d), along_x(d)))
    second = total[0]
    for d in range(1, RING):
        second = second + moved(total[d], by_core(along_x(d), along_y(d)))
    third = lax.dynamic_slice_in_dim(second, z * 36, 36, 0)
    for d in range(1, RING):
        share = lax.dynamic_slice_in_dim(second, (z + d) % RING * 36, 36, 0)
        third = third + moved(share, along_z(d))
    own = lax.dynamic_slice_in_dim(third, c * 18, 18, 0)
    give = moved(lax.dynamic_slice_in_dim(third, (1 - c) * 18, 18, 0), partner)
    return (jnp.where(first, own, give), jnp.where(first, give, own))


def solution(mesh):
    split = Mesh(mesh.devices.reshape(SIZES), AXES)
    rows, cols = P(DP, None), P(DP, "yh")
    return jax.shard_map(
        per_device,
        mesh=split,
        in_specs=(rows, rows, cols, cols, P(), P()),
        out_specs=(cols, cols),
        check_vma=False,
    )
```

```python
import jax
import jax.numpy as jnp
from jax import lax
from jax.experimental import pallas as pl
from jax.experimental.pallas import tpu as pltpu
from jax.sharding import Mesh
from jax.sharding import PartitionSpec as P

SHIFTS = 4
DP = ("yl", "x", "z", "c")
AXES = ("yl", "x", "z", "c", "yh")
SIZES = (2, 4, 4, 2, 2)
RING = 4
WIDE = 512
D = 1152
BAND = 144
UPPER = 80
PIECE = 656
IMG_ROWS = 768
TXT_ROWS = 384
ROWS = IMG_ROWS + SHIFTS * TXT_ROWS
CHUNK = 256

epsilon = 1e-06
f32 = jnp.float32
bf16 = jnp.bfloat16


def place(yl, x, z, c, yh):
    at = 0
    for coordinate, size in zip((yl, x, z, c, yh), SIZES):
        at = at * size + coordinate
    return at


def moved(array, target):
    pairs = []
    for yl in range(2):
        for x in range(4):
            for z in range(4):
                for c in range(2):
                    for yh in range(2):
                        pairs.append((place(yl, x, z, c, yh), place(*target(yl, x, z, c, yh))))
    return lax.ppermute(array, AXES, pairs)


def along_x(d):
    return lambda yl, x, z, c, yh: (yl, (x + d) % 4, z, c, yh)


def along_y(d):
    def to(yl, x, z, c, yh):
        y = (yh * 2 + yl + d) % 4
        return (y % 2, x, z, c, y // 2)

    return to


def along_z(d):
    return lambda yl, x, z, c, yh: (yl, x, (z + d) % 4, c, yh)


def partner(yl, x, z, c, yh):
    return (yl, x, z, 1 - c, yh)


def by_core(zero, one):
    return lambda yl, x, z, c, yh: (one if c else zero)(yl, x, z, c, yh)


def next_block(yl, x, z, c, yh):
    k = (((yl * 4 + x) * 4 + z) * 2 + c + 1) % 64
    return (k // 32, k // 8 % 4, k // 2 % 4, k % 2, yh)


def tdot(left, right):
    return lax.dot_general(left, right, (((0,), (0,)), ((), ())), preferred_element_type=f32)


def rdot(left, right):
    return lax.dot_general(left, right, (((1,), (1,)), ((), ())), preferred_element_type=f32)


def position(role, x, y, near, far):
    px = jnp.where(role == 0, (x + near) % 4, (x + far) % 4)
    py = jnp.where(role == 0, (y + far) % 4, (y + near) % 4)
    return px, py


def aligned(start, size, step):
    return pl.ds(pl.multiple_of(start, step), size)


def joined(upper, lower):
    return jnp.concatenate([upper, lower], axis=1)


def projected(feats, heads, units, lows, scales, scale):
    def step(i, _):
        rows = aligned(i * CHUNK, CHUNK, CHUNK)
        base = jnp.where(i * CHUNK >= IMG_ROWS, D, 0)
        square = jnp.zeros((CHUNK, 1), f32)
        for start in range(0, D, 256):
            width = min(256, D - start)
            cols = slice(start, start + width)
            proj = jnp.dot(
                feats[rows, :], heads[aligned(base, D, D), cols], preferred_element_type=f32
            )
            units[rows, cols] = proj
            square = square + jnp.sum(proj * proj, axis=1, keepdims=True)
        inverse = 1.0 / jnp.sqrt(square + epsilon)
        scales[rows, :] = jnp.broadcast_to(inverse * scale, (CHUNK, 128))
        unit = units[rows, :] * inverse
        units[rows, :] = unit
        lows[rows, :] = unit.astype(bf16)
        return 0

    lax.fori_loop(0, ROWS // CHUNK, step, 0)


def before(units, scales, rows, grad):
    unit = units[rows, :]
    inner = jnp.sum(unit * grad, axis=1, keepdims=True)
    return ((grad - unit * inner) * scales[rows, :1]).astype(bf16)


def local_kernel(at, scalars, *refs):
    pieces, feats_in, flipped_in = refs[:8], refs[8:13], refs[13:18]
    kept, sent = refs[18:20]
    held, feats, img_flipped, txt_flipped, heads, units, lows, scales, weights, staged = refs[20:30]
    sem_pieces, sem_feats, sem_flipped, sem_out = refs[30:]
    c, x, y = at[0], at[1], at[2]
    scale, bias = scalars[0], scalars[1]

    loads = [pltpu.make_async_copy(p, held.at[i], sem_pieces.at[i]) for i, p in enumerate(pieces)]
    feat_loads, flip_loads = [], []
    for i in range(5):
        size = IMG_ROWS if i == 0 else TXT_ROWS
        start = 0 if i == 0 else IMG_ROWS + (i - 1) * TXT_ROWS
        feat_loads.append(
            pltpu.make_async_copy(feats_in[i], feats.at[pl.ds(start, size)], sem_feats.at[i])
        )
        target = img_flipped if i == 0 else txt_flipped.at[:, pl.ds((i - 1) * TXT_ROWS, TXT_ROWS)]
        flip_loads.append(pltpu.make_async_copy(flipped_in[i], target, sem_flipped.at[i]))
    for copy in loads + feat_loads + flip_loads:
        copy.start()
    for copy in loads:
        copy.wait()

    def put(i, _):
        source, far, near = i // 16, i // 4 % 4, i % 4
        role = jnp.where(source == 0, c, 1 - c)
        px, py = position(role, x, y, near, far)
        start = role * D + (py % 2 * 4 + px) * BAND
        for half in range(2):

            @pl.when(py // 2 == half)
            def _():
                for q in range(4):
                    cols = slice(half * WIDE + q * 128, half * WIDE + q * 128 + 128)
                    heads[aligned(start, BAND, BAND), cols] = held[
                        source * 4 + far, near, q * BAND : (q + 1) * BAND, :
                    ]
                tail = held[source * 4 + far, near, 4 * BAND :, :]
                cols = slice(2 * WIDE + half * 64, 2 * WIDE + half * 64 + 64)
                heads[aligned(start, UPPER, 16), cols] = tail[:, :64]
                heads[aligned(start + UPPER, BAND - UPPER, 16), cols] = tail[: BAND - UPPER, 64:]

        return 0

    lax.fori_loop(0, 32, put, 0)
    for copy in feat_loads:
        copy.wait()
    projected(feats, heads, units, lows, scales, scale)
    before_rows = heads

    def tile(t, _):
        rows = aligned(IMG_ROWS + t * TXT_ROWS, TXT_ROWS, 128)
        cols = aligned(t * TXT_ROWS, TXT_ROWS, 128)
        low = lows[rows, :]

        def part(i, _):
            img_rows = aligned(i * 256, 256, 256)
            logits = scale * rdot(lows[img_rows, :], low) + bias
            r = lax.broadcasted_iota(jnp.int32, logits.shape, 0) + i * 256
            k = lax.broadcasted_iota(jnp.int32, logits.shape, 1) + y // 2 * TXT_ROWS
            half = jnp.where((r == k) & (t == 0), -0.5, 0.5)
            share = 0.5 * jnp.tanh(half * logits) + 0.5
            weights[img_rows, cols] = (2.0 * half * share).astype(bf16)
            return 0

        lax.fori_loop(0, IMG_ROWS // 256, part, 0)
        grad = tdot(weights[:, cols], lows[:IMG_ROWS, :])
        before_rows[rows, :] = before(units, scales, rows, grad)
        return 0

    lax.fori_loop(0, SHIFTS, tile, 0)

    def image(i, _):
        rows = aligned(i * CHUNK, CHUNK, CHUNK)
        grad = jnp.dot(weights[rows, :], lows[IMG_ROWS:, :], preferred_element_type=f32)
        before_rows[rows, :] = before(units, scales, rows, grad)
        return 0

    lax.fori_loop(0, IMG_ROWS // CHUNK, image, 0)
    for copy in flip_loads:
        copy.wait()

    def stores(head, near_half, slot):
        copies = []
        for px in range(4):
            for half in range(2):
                dy = (half * 2 + near_half + 4 - y) % 4
                dx = (px + 4 - x) % 4
                near, far = (dy, dx) if head == 0 else (dx, dy)
                target = lambda out: out.at[near, far]
                copies.append(
                    [
                        pltpu.make_async_copy(
                            staged.at[slot, px * 2 + half], target(out), sem_out.at[slot, px * 2 + half]
                        )
                        for out in (kept, sent)
                    ]
                )
        return copies

    groups = []
    for head in range(2):
        flipped = img_flipped if head == 0 else txt_flipped
        source = slice(0, IMG_ROWS) if head == 0 else slice(IMG_ROWS, ROWS)
        for near_half in range(2):
            slot = len(groups) % 2
            if len(groups) >= 2:
                for copy in groups[-2]:
                    copy[0].wait()
            left = slice(near_half * 4 * BAND, near_half * 4 * BAND + 4 * BAND)

            def wide(n, _, flipped=flipped, source=source, left=left, slot=slot):
                cols = aligned(n * 256, 256, 256)
                total = jnp.dot(
                    flipped[left, :], before_rows[source, cols], preferred_element_type=f32
                )
                half = n // 2
                first = pl.multiple_of(n % 2 * 2 * BAND, BAND)
                for px in range(4):
                    for q in range(2):
                        staged[slot, px * 2 + half, pl.ds(first + q * BAND, BAND), :] = total[
                            px * BAND : (px + 1) * BAND, q * 128 : (q + 1) * 128
                        ]
                return 0

            lax.fori_loop(0, 4, wide, 0)
            total = jnp.dot(
                flipped[left, :], before_rows[source, 2 * WIDE :], preferred_element_type=f32
            )
            for px in range(4):
                for half in range(2):
                    lanes = slice(half * 64, half * 64 + 64)
                    upper = total[px * BAND : px * BAND + UPPER, lanes]
                    lower = jnp.concatenate(
                        [
                            total[px * BAND + UPPER : (px + 1) * BAND, lanes],
                            jnp.zeros((2 * UPPER - BAND, 64), f32),
                        ],
                        axis=0,
                    )
                    staged[slot, px * 2 + half, 4 * BAND :, :] = joined(upper, lower)
            group = stores(head, near_half, slot)
            for which in range(2):

                @pl.when(c == (head if which == 0 else 1 - head))
                def _():
                    for copy in group:
                        copy[which].start()

            groups.append(group)
    for group in groups[-2:]:
        for copy in group:
            copy[0].wait()


def local(at, scalars, pieces, feats, flipped):
    anywhere = pl.BlockSpec(memory_space=pl.ANY)
    smem = pl.BlockSpec(memory_space=pltpu.SMEM)
    result = jax.ShapeDtypeStruct((RING, RING, PIECE, 128), f32)
    return pl.pallas_call(
        local_kernel,
        out_shape=[result, result],
        in_specs=[smem, smem] + [anywhere] * 18,
        out_specs=[anywhere] * 2,
        scratch_shapes=[
            pltpu.VMEM((8, RING, PIECE, 128), bf16),
            pltpu.VMEM((ROWS, D), bf16),
            pltpu.VMEM((D, IMG_ROWS), bf16),
            pltpu.VMEM((D, SHIFTS * TXT_ROWS), bf16),
            pltpu.VMEM((ROWS, D), bf16),
            pltpu.VMEM((ROWS, D), f32),
            pltpu.VMEM((ROWS, D), bf16),
            pltpu.VMEM((ROWS, 128), f32),
            pltpu.VMEM((IMG_ROWS, SHIFTS * TXT_ROWS), bf16),
            pltpu.VMEM((2, 8, PIECE, 128), f32),
            pltpu.SemaphoreType.DMA((8,)),
            pltpu.SemaphoreType.DMA((5,)),
            pltpu.SemaphoreType.DMA((5,)),
            pltpu.SemaphoreType.DMA((2, 8)),
        ],
        compiler_params=pltpu.CompilerParams(vmem_limit_bytes=60 * 2**20),
        cost_estimate=pl.CostEstimate(
            flops=20_400_000_000, bytes_accessed=27_000_000, transcendentals=1_200_000
        ),
        name="local",
    )(at, scalars, *pieces, *feats, *flipped)


def packed_piece(piece):
    tail = jnp.pad(piece[UPPER:, WIDE:], ((0, 2 * UPPER - BAND), (0, 0)))
    return jnp.concatenate(
        [piece[:, q * 128 : (q + 1) * 128] for q in range(4)]
        + [joined(piece[:UPPER, WIDE:], tail)],
        axis=0,
    )


def unpacked_piece(piece):
    tail = piece[4 * BAND :]
    tail = jnp.concatenate([tail[:, :64], tail[: BAND - UPPER, 64:]], axis=0)
    return jnp.concatenate([piece[q * BAND : (q + 1) * BAND] for q in range(4)] + [tail], axis=1)


def rolled(parts, index, rows):
    twice = jnp.concatenate(parts + parts, axis=0)
    return lax.dynamic_slice_in_dim(twice, (RING - index) % RING * rows, RING * rows, 0)


def per_device(img_feat, txt_feat, img_head, txt_head, logit_scale, logit_bias):
    yl, x, z, c, yh = (lax.axis_index(a) for a in AXES)
    y = yh * 2 + yl
    at = jnp.stack([c, x, y]).astype(jnp.int32)

    first = c == 0
    mine = jnp.where(first, img_head, txt_head)
    come = moved(jnp.where(first, txt_head, img_head), partner)
    rows36 = jnp.where(
        first, jnp.concatenate([mine, come], 0), jnp.concatenate([come, mine], 0)
    )
    parts = [rows36] + [moved(rows36, along_z(-d)) for d in range(1, RING)]
    piece = packed_piece(rolled(parts, z, 36))

    piece, txt_feat = lax.optimization_barrier((piece, txt_feat))
    visitors = [lax.dynamic_slice_in_dim(txt_feat, yh * TXT_ROWS, TXT_ROWS, 0)]
    for _ in range(1, SHIFTS):
        visitors.append(moved(visitors[-1], next_block))
    feats = [img_feat] + visitors
    flipped = [f.T for f in feats]

    near = [piece] + [moved(piece, by_core(along_x(-d), along_y(-d))) for d in range(1, RING)]
    near = jnp.stack(near)
    far = [near] + [moved(near, by_core(along_y(-d), along_x(-d))) for d in range(1, RING)]
    other = [moved(a, partner) for a in far]
    scalars = jnp.concatenate([logit_scale, logit_bias])
    kept, sent = local(at, scalars, far + other, feats, flipped)

    come = moved(sent, partner)
    total = kept[0] + come[0]
    for d in range(1, RING):
        share = (kept[d] + come[d]).astype(bf16)
        total = total + moved(share, by_core(along_y(d), along_x(d))).astype(f32)
    second = total[0]
    for d in range(1, RING):
        second = second + moved(total[d], by_core(along_x(d), along_y(d)))
    second = unpacked_piece(second)
    third = lax.dynamic_slice_in_dim(second, z * 36, 36, 0)
    for d in range(1, RING):
        share = lax.dynamic_slice_in_dim(second, (z + d) % RING * 36, 36, 0)
        third = third + moved(share, along_z(d))
    own = lax.dynamic_slice_in_dim(third, c * 18, 18, 0)
    give = moved(lax.dynamic_slice_in_dim(third, (1 - c) * 18, 18, 0), partner)
    return (jnp.where(first, own, give), jnp.where(first, give, own))


def solution(mesh):
    split = Mesh(mesh.devices.reshape(SIZES), AXES)
    rows, cols = P(DP, None), P(DP, "yh")
    return jax.shard_map(
        per_device,
        mesh=split,
        in_specs=(rows, rows, cols, cols, P(), P()),
        out_specs=(cols, cols),
        check_vma=False,
    )
```

```python
import jax
import jax.numpy as jnp
from jax import lax
from jax.experimental import pallas as pl
from jax.experimental.pallas import tpu as pltpu
from jax.sharding import Mesh
from jax.sharding import PartitionSpec as P

SHIFTS = 4
DP = ("yl", "x", "z", "c")
AXES = ("yl", "x", "z", "c", "yh")
SIZES = (2, 4, 4, 2, 2)
RING = 4
WIDE = 512
D = 1152
BAND = 144
UPPER = 80
PIECE = 656
BLOCK = 768
OTHERS = SHIFTS * BLOCK
ROWS = BLOCK + OTHERS
SHARE = 36
PART = 328
CHUNK = 384

epsilon = 1e-06
f32 = jnp.float32
bf16 = jnp.bfloat16


def place(yl, x, z, c, yh):
    at = 0
    for coordinate, size in zip((yl, x, z, c, yh), SIZES):
        at = at * size + coordinate
    return at


def moved(array, target):
    pairs = []
    for yl in range(2):
        for x in range(4):
            for z in range(4):
                for c in range(2):
                    for yh in range(2):
                        end = target(yl, x, z, c, yh)
                        if end is not None:
                            pairs.append((place(yl, x, z, c, yh), place(*end)))
    return lax.ppermute(array, AXES, pairs)


def along_x(d):
    return lambda yl, x, z, c, yh: (yl, (x + d) % 4, z, c, yh)


def along_y(d):
    def to(yl, x, z, c, yh):
        y = (yh * 2 + yl + d) % 4
        return (y % 2, x, z, c, y // 2)

    return to


def along_z(d):
    return lambda yl, x, z, c, yh: (yl, x, (z + d) % 4, c, yh)


def partner(yl, x, z, c, yh):
    return (yl, x, z, 1 - c, yh)


def by_core(zero, one):
    return lambda yl, x, z, c, yh: (one if c else zero)(yl, x, z, c, yh)


def mirrored(to):
    def both(yl, x, z, c, yh):
        at = (yl, x, z, c) if yh == 0 else (1 - yl, 3 - x, 3 - z, 1 - c)
        end = to(*at)
        if end is None:
            return None
        yl, x, z, c = end if yh == 0 else (1 - end[0], 3 - end[1], 3 - end[2], 1 - end[3])
        return (yl, x, z, c, yh)

    return both


def two_on(yl, x, z, c):
    chip = ((yl * 4 + x) * 4 + z + 1) % 32
    return (chip // 16, chip // 4 % 4, chip % 4, c)


def first_leg(yl, x, z, c):
    return (yl, x, z, 1) if c == 0 else (yl, x, (z - 1) % 4, 0)


def second_leg(yl, x, z, c):
    if c == 1:
        return None
    chip = ((yl * 4 + x) * 4 + (z + 1) % 4 + 2) % 32
    return (chip // 16, chip // 4 % 4, chip % 4, 0)


def to_owner(a, b):
    return lambda yl, x, z, c, yh: (c, x, z, yl ^ a, yh ^ b)


def tdot(left, right):
    return lax.dot_general(left, right, (((0,), (0,)), ((), ())), preferred_element_type=f32)


def rdot(left, right):
    return lax.dot_general(left, right, (((1,), (1,)), ((), ())), preferred_element_type=f32)


def position(role, x, y, near, far):
    px = jnp.where(role == 0, (x + near) % 4, (x + far) % 4)
    py = jnp.where(role == 0, (y + far) % 4, (y + near) % 4)
    return px, py


def aligned(start, size, step):
    return pl.ds(pl.multiple_of(start, step), size)


def joined(upper, lower):
    return jnp.concatenate([upper, lower], axis=1)


def before(units, scales, rows, grad):
    unit = units[rows, :]
    inner = jnp.sum(unit * grad, axis=1, keepdims=True)
    return ((grad - unit * inner) * scales[rows, :1]).astype(bf16)


def local_kernel(at, scalars, *refs):
    pieces, (img_in, txt_in, two_in, swapped_in, near_in, far_in) = refs[:8], refs[8:14]
    kept, sent = refs[14:16]
    held, feats, flipped, heads, units, lows, scales, weights, rounded, staged = refs[16:26]
    raws, scores = refs[26:28], refs[28:30]
    sem_pieces, sem_feats, sem_out = refs[30:]
    c, x, y, z = at[0], at[1], at[2], at[3]
    side = y // 2
    scale, bias = scalars[0], scalars[1]

    loads = [pltpu.make_async_copy(p, held.at[i], sem_pieces.at[i]) for i, p in enumerate(pieces)]
    for copy in loads:
        copy.start()

    def feat_load(i, source):
        return pltpu.make_async_copy(source, feats.at[pl.ds(i * BLOCK, BLOCK)], sem_feats.at[i])

    for copy in loads:
        copy.wait()
    for which, (own, other) in enumerate(((img_in, txt_in), (txt_in, img_in))):

        @pl.when(side == which)
        def _():
            feat_load(0, own).start()
            feat_load(1, other).start()

    feat_load(2, two_in).start()
    feat_load(3, swapped_in).start()
    for which, source in enumerate((far_in, near_in)):

        @pl.when((c + side) % 2 == which)
        def _():
            feat_load(4, source).start()

    def put(i, _):
        source, far, near = i // 16, i // 4 % 4, i % 4
        role = jnp.where(source == 0, c, 1 - c)
        px, py = position(role, x, y, near, far)
        start = role * D + (py % 2 * 4 + px) * BAND
        for half in range(2):

            @pl.when(py // 2 == half)
            def _():
                for q in range(4):
                    cols = slice(half * WIDE + q * 128, half * WIDE + q * 128 + 128)
                    heads[aligned(start, BAND, BAND), cols] = held[
                        source * 4 + far, near, q * BAND : (q + 1) * BAND, :
                    ]
                tail = held[source * 4 + far, near, 4 * BAND :, :]
                cols = slice(2 * WIDE + half * 64, 2 * WIDE + half * 64 + 64)
                heads[aligned(start, UPPER, 16), cols] = tail[:, :64]
                heads[aligned(start + UPPER, BAND - UPPER, 16), cols] = tail[: BAND - UPPER, 64:]

        return 0

    lax.fori_loop(0, 32, put, 0)
    for i, source in enumerate((img_in, txt_in, two_in, swapped_in, far_in)):
        feat_load(i, source).wait()

    own_base = pl.multiple_of(side * D, D)
    other_base = pl.multiple_of((1 - side) * D, D)

    def project(i, raw, base):
        rows = aligned(i * CHUNK, CHUNK, CHUNK)
        for start in range(0, D, 256):
            width = min(256, D - start)
            cols = slice(start, start + width)
            raw[:, cols] = jnp.dot(
                feats[rows, :], heads[pl.ds(base, D), cols], preferred_element_type=f32
            )

    def finish(i, raw, own=False):
        rows = aligned(i * CHUNK, CHUNK, CHUNK)
        proj = raw[...]
        square = jnp.sum(proj * proj, axis=1, keepdims=True)
        inverse = 1.0 / jnp.sqrt(square + epsilon)
        unit = proj * inverse
        lows[rows, :] = unit.astype(bf16)
        if own:
            units[rows, :] = unit
            scales[rows, :] = jnp.broadcast_to(inverse * scale, (CHUNK, 128))
            flipped[:, rows] = feats[rows, :].T

    project(0, raws[0], own_base)

    def own_step(i, raw, after, base):
        finish(i, raw, own=True)
        project(i + 1, after, base)

    own_step(0, raws[0], raws[1], own_base)
    own_step(1, raws[1], raws[0], other_base)

    def two(j, _):
        finish(2 * j + 2, raws[0])
        project(2 * j + 3, raws[1], other_base)
        finish(2 * j + 3, raws[1])
        project(2 * j + 4, raws[0], other_base)
        return 0

    lax.fori_loop(0, 3, two, 0)
    finish(8, raws[0])
    project(9, raws[1], other_base)
    finish(9, raws[1])

    def score(t, to):
        rows = aligned(BLOCK + t * CHUNK, CHUNK, CHUNK)
        to[...] = rdot(lows[:BLOCK, :], lows[rows, :])

    def weigh(t, came, own=False):
        logits = scale * came[...] + bias
        half = 0.5
        if own:
            r = lax.broadcasted_iota(jnp.int32, logits.shape, 0)
            k = lax.broadcasted_iota(jnp.int32, logits.shape, 1) + t * CHUNK
            half = jnp.where(r == k, -0.5, 0.5)
        share = 0.5 * jnp.tanh(half * logits) + 0.5
        share = 2.0 * half * share if own else share
        weights[:, aligned(t * CHUNK, CHUNK, CHUNK)] = share.astype(bf16)

    score(0, scores[0])
    weigh(0, scores[0], own=True)
    score(1, scores[1])
    weigh(1, scores[1], own=True)
    score(2, scores[0])

    def pair(j, _):
        weigh(2 * j + 2, scores[0])
        score(2 * j + 3, scores[1])
        weigh(2 * j + 3, scores[1])
        score(2 * j + 4, scores[0])
        return 0

    lax.fori_loop(0, 2, pair, 0)
    weigh(6, scores[0])
    score(7, scores[1])
    weigh(7, scores[1])

    def gradient(i, _):
        rows = aligned(i * 192, 192, 192)
        grad = jnp.dot(weights[rows, :], lows[BLOCK:, :], preferred_element_type=f32)
        rounded[rows, :] = before(units, scales, rows, grad)
        return 0

    lax.fori_loop(0, BLOCK // 192, gradient, 0)

    for half in range(2):
        left = slice(half * D // 2, (half + 1) * D // 2)
        for start in range(0, D, 256):
            width = min(256, D - start)
            total = jnp.dot(
                flipped[left, :], rounded[:, start : start + width], preferred_element_type=f32
            )
            for px in range(4):
                for pz in range(4):
                    dx, dz = (px + 4 - x) % 4, (pz + 4 - z) % 4
                    near, far = (dx, dz) if half == 0 else (dz, dx)
                    row = (px * 4 + pz) * SHARE
                    for q in range(width // 128):
                        to = (start // 128 + q) * SHARE
                        staged[half, near, far, to : to + SHARE, :] = total[
                            row : row + SHARE, q * 128 : (q + 1) * 128
                        ]
        for which, out in enumerate((kept, sent)):

            @pl.when(c == (half if which == 0 else 1 - half))
            def _():
                pltpu.make_async_copy(staged.at[half], out, sem_out.at[half]).start()

    for half in range(2):
        pltpu.make_async_copy(staged.at[half], kept, sem_out.at[half]).wait()


def local(at, scalars, pieces, feats):
    anywhere = pl.BlockSpec(memory_space=pl.ANY)
    smem = pl.BlockSpec(memory_space=pltpu.SMEM)
    result = jax.ShapeDtypeStruct((RING, RING, PART, 128), f32)
    return pl.pallas_call(
        local_kernel,
        out_shape=[result, result],
        in_specs=[smem, smem] + [anywhere] * 14,
        out_specs=[anywhere] * 2,
        scratch_shapes=[
            pltpu.VMEM((8, RING, PIECE, 128), bf16),
            pltpu.VMEM((ROWS, D), bf16),
            pltpu.VMEM((D, BLOCK), bf16),
            pltpu.VMEM((2 * D, D), bf16),
            pltpu.VMEM((BLOCK, D), f32),
            pltpu.VMEM((ROWS, D), bf16),
            pltpu.VMEM((BLOCK, 128), f32),
            pltpu.VMEM((BLOCK, OTHERS), bf16),
            pltpu.VMEM((BLOCK, D), bf16),
            pltpu.VMEM((2, RING, RING, PART, 128), f32),
            pltpu.VMEM((CHUNK, D), f32),
            pltpu.VMEM((CHUNK, D), f32),
            pltpu.VMEM((BLOCK, CHUNK), f32),
            pltpu.VMEM((BLOCK, CHUNK), f32),
            pltpu.SemaphoreType.DMA((8,)),
            pltpu.SemaphoreType.DMA((5,)),
            pltpu.SemaphoreType.DMA((2,)),
        ],
        compiler_params=pltpu.CompilerParams(vmem_limit_bytes=62 * 2**20),
        cost_estimate=pl.CostEstimate(
            flops=23_100_000_000, bytes_accessed=20_000_000, transcendentals=2_400_000
        ),
        name="local",
    )(at, scalars, *pieces, *feats)


def packed_piece(piece):
    tail = jnp.pad(piece[UPPER:, WIDE:], ((0, 2 * UPPER - BAND), (0, 0)))
    return jnp.concatenate(
        [piece[:, q * 128 : (q + 1) * 128] for q in range(4)]
        + [joined(piece[:UPPER, WIDE:], tail)],
        axis=0,
    )


def rolled(parts, index, rows):
    twice = jnp.concatenate(parts + parts, axis=0)
    return lax.dynamic_slice_in_dim(twice, (RING - index) % RING * rows, RING * rows, 0)


def per_device(img_feat, txt_feat, img_head, txt_head, logit_scale, logit_bias):
    yl, x, z, c, yh = (lax.axis_index(a) for a in AXES)
    y = yh * 2 + yl
    at = jnp.stack([c, x, y, z]).astype(jnp.int32)

    first = c == 0
    mine = jnp.where(first, img_head, txt_head)
    come = moved(jnp.where(first, txt_head, img_head), partner)
    rows36 = jnp.where(
        first, jnp.concatenate([mine, come], 0), jnp.concatenate([come, mine], 0)
    )
    parts = [rows36] + [moved(rows36, along_z(-d)) for d in range(1, RING)]
    piece = packed_piece(rolled(parts, z, 36))

    other_feat = jnp.where(yh == 0, txt_feat, img_feat)
    piece, other_feat = lax.optimization_barrier((piece, other_feat))
    two_back = moved(other_feat, mirrored(two_on))
    next_leg = moved(other_feat, mirrored(first_leg))

    near = [piece] + [moved(piece, by_core(along_x(-d), along_y(-d))) for d in range(1, RING)]
    near = jnp.stack(near)
    far = [near] + [moved(near, by_core(along_y(-d), along_x(-d))) for d in range(1, RING)]
    leg, _ = lax.optimization_barrier((next_leg, far[1]))
    last_leg = moved(leg, mirrored(second_leg))
    two_back, _ = lax.optimization_barrier((two_back, far[3]))
    swapped = moved(two_back, partner)
    other = [moved(a, partner) for a in far]
    scalars = jnp.concatenate([logit_scale, logit_bias])
    feats = [img_feat, txt_feat, two_back, swapped, next_leg, last_leg]
    kept, sent = local(at, scalars, far + other, feats)

    come = moved(sent, partner)
    total = kept[0] + come[0]
    for d in range(1, RING):
        share = (kept[d] + come[d]).astype(bf16)
        total = total + moved(share, by_core(along_x(d), along_z(d))).astype(f32)
    second = total[0]
    for d in range(1, RING):
        second = second + moved(total[d], by_core(along_z(d), along_x(d)))
    chunks = [second[q * SHARE : (q + 1) * SHARE] for q in range(9)]
    halves = [
        jnp.concatenate(chunks[4 * h : 4 * h + 4] + [chunks[8][:, h * 64 : h * 64 + 64]], axis=1)
        for h in range(2)
    ]
    results = []
    for b in range(2):
        half = jnp.where(yh ^ b == 0, halves[0], halves[1])
        result = 0.0
        for a in range(2):
            share = lax.dynamic_slice_in_dim(half, (yl ^ a) * 18, 18, 0)
            result = result + moved(share, to_owner(a, b))
        results.append(result)
    return (
        jnp.where(yh == 0, results[0], results[1]),
        jnp.where(yh == 0, results[1], results[0]),
    )


def solution(mesh):
    split = Mesh(mesh.devices.reshape(SIZES), AXES)
    rows, cols = P(DP, None), P(DP, "yh")
    return jax.shard_map(
        per_device,
        mesh=split,
        in_specs=(rows, rows, cols, cols, P(), P()),
        out_specs=(cols, cols),
        check_vma=False,
    )
```

```python
import jax
import jax.numpy as jnp
from jax import lax
from jax.experimental import pallas as pl
from jax.experimental.pallas import tpu as pltpu
from jax.sharding import Mesh
from jax.sharding import PartitionSpec as P

SHIFTS = 4
DP = ("yl", "x", "z", "c")
AXES = ("yl", "x", "z", "c", "yh")
SIZES = (2, 4, 4, 2, 2)
RING = 4
WIDE = 512
D = 1152
BAND = 144
UPPER = 80
PIECE = 656
BLOCK = 768
OTHERS = SHIFTS * BLOCK
ROWS = BLOCK + OTHERS
SHARE = 36
PART = 328
CHUNK = 384

epsilon = 1e-06
f32 = jnp.float32
bf16 = jnp.bfloat16


def place(yl, x, z, c, yh):
    at = 0
    for coordinate, size in zip((yl, x, z, c, yh), SIZES):
        at = at * size + coordinate
    return at


def moved(array, target):
    pairs = []
    for yl in range(2):
        for x in range(4):
            for z in range(4):
                for c in range(2):
                    for yh in range(2):
                        end = target(yl, x, z, c, yh)
                        if end is not None:
                            pairs.append((place(yl, x, z, c, yh), place(*end)))
    return lax.ppermute(array, AXES, pairs)


def along_x(d):
    return lambda yl, x, z, c, yh: (yl, (x + d) % 4, z, c, yh)


def along_y(d):
    def to(yl, x, z, c, yh):
        y = (yh * 2 + yl + d) % 4
        return (y % 2, x, z, c, y // 2)

    return to


def along_z(d):
    return lambda yl, x, z, c, yh: (yl, x, (z + d) % 4, c, yh)


def partner(yl, x, z, c, yh):
    return (yl, x, z, 1 - c, yh)


def by_core(zero, one):
    return lambda yl, x, z, c, yh: (one if c else zero)(yl, x, z, c, yh)


def mirrored(to):
    def both(yl, x, z, c, yh):
        at = (yl, x, z, c) if yh == 0 else (1 - yl, 3 - x, 3 - z, 1 - c)
        end = to(*at)
        if end is None:
            return None
        yl, x, z, c = end if yh == 0 else (1 - end[0], 3 - end[1], 3 - end[2], 1 - end[3])
        return (yl, x, z, c, yh)

    return both


def two_on(yl, x, z, c):
    chip = ((yl * 4 + x) * 4 + z + 1) % 32
    return (chip // 16, chip // 4 % 4, chip % 4, c)


def first_leg(yl, x, z, c):
    return (yl, x, z, 1) if c == 0 else (yl, x, (z - 1) % 4, 0)


def second_leg(yl, x, z, c):
    if c == 1:
        return None
    chip = ((yl * 4 + x) * 4 + (z + 1) % 4 + 2) % 32
    return (chip // 16, chip // 4 % 4, chip % 4, 0)


def to_owner(a, b):
    return lambda yl, x, z, c, yh: (c, x, z, yl ^ a, yh ^ b)


def tdot(left, right):
    return lax.dot_general(left, right, (((0,), (0,)), ((), ())), preferred_element_type=f32)


def rdot(left, right):
    return lax.dot_general(left, right, (((1,), (1,)), ((), ())), preferred_element_type=f32)


def position(role, x, y, near, far):
    px = jnp.where(role == 0, (x + near) % 4, (x + far) % 4)
    py = jnp.where(role == 0, (y + far) % 4, (y + near) % 4)
    return px, py


def aligned(start, size, step):
    return pl.ds(pl.multiple_of(start, step), size)


def joined(upper, lower):
    return jnp.concatenate([upper, lower], axis=1)


def before(units, scales, rows, grad):
    unit = units[rows, :]
    inner = jnp.sum(unit * grad, axis=1, keepdims=True)
    return ((grad - unit * inner) * scales[rows, :1]).astype(bf16)


def local_kernel(at, scalars, *refs):
    pieces, (img_in, txt_in, near_in, far_in), halves_in = refs[:8], refs[8:12], refs[12:16]
    kept, sent = refs[16:18]
    held, feats, flipped, heads, units, lows, scales, weights, rounded, staged = refs[18:28]
    raws, scores = refs[28:30], refs[30:32]
    sem_pieces, sem_feats, sem_halves, sem_out = refs[32:]
    c, x, y, z = at[0], at[1], at[2], at[3]
    side = y // 2
    scale, bias = scalars[0], scalars[1]

    loads = [pltpu.make_async_copy(p, held.at[i], sem_pieces.at[i]) for i, p in enumerate(pieces)]
    for copy in loads:
        copy.start()

    def feat_load(i, source):
        return pltpu.make_async_copy(source, feats.at[pl.ds(i * BLOCK, BLOCK)], sem_feats.at[i])

    for copy in loads:
        copy.wait()
    for which, (own, other) in enumerate(((img_in, txt_in), (txt_in, img_in))):

        @pl.when(side == which)
        def _():
            feat_load(0, own).start()
            feat_load(1, other).start()

    half_loads = [
        pltpu.make_async_copy(
            source, feats.at[pl.ds(2 * BLOCK + i * CHUNK, CHUNK)], sem_halves.at[i]
        )
        for i, source in enumerate(halves_in)
    ]
    for copy in half_loads:
        copy.start()
    for which, source in enumerate((far_in, near_in)):

        @pl.when((c + side) % 2 == which)
        def _():
            feat_load(4, source).start()

    def put(i, _):
        source, far, near = i // 16, i // 4 % 4, i % 4
        role = jnp.where(source == 0, c, 1 - c)
        px, py = position(role, x, y, near, far)
        start = role * D + (py % 2 * 4 + px) * BAND
        for half in range(2):

            @pl.when(py // 2 == half)
            def _():
                for q in range(4):
                    cols = slice(half * WIDE + q * 128, half * WIDE + q * 128 + 128)
                    heads[aligned(start, BAND, BAND), cols] = held[
                        source * 4 + far, near, q * BAND : (q + 1) * BAND, :
                    ]
                tail = held[source * 4 + far, near, 4 * BAND :, :]
                cols = slice(2 * WIDE + half * 64, 2 * WIDE + half * 64 + 64)
                heads[aligned(start, UPPER, 16), cols] = tail[:, :64]
                heads[aligned(start + UPPER, BAND - UPPER, 16), cols] = tail[: BAND - UPPER, 64:]

        return 0

    lax.fori_loop(0, 32, put, 0)
    for i in (0, 1, 4):
        feat_load(i, far_in).wait()
    for copy in half_loads:
        copy.wait()

    own_base = pl.multiple_of(side * D, D)
    other_base = pl.multiple_of((1 - side) * D, D)

    def project(i, raw, base):
        rows = aligned(i * CHUNK, CHUNK, CHUNK)
        for start in range(0, D, 256):
            width = min(256, D - start)
            cols = slice(start, start + width)
            raw[:, cols] = jnp.dot(
                feats[rows, :], heads[pl.ds(base, D), cols], preferred_element_type=f32
            )

    def finish(i, raw, own=False):
        rows = aligned(i * CHUNK, CHUNK, CHUNK)
        proj = raw[...]
        square = jnp.sum(proj * proj, axis=1, keepdims=True)
        inverse = 1.0 / jnp.sqrt(square + epsilon)
        unit = proj * inverse
        lows[rows, :] = unit.astype(bf16)
        if own:
            units[rows, :] = unit
            scales[rows, :] = jnp.broadcast_to(inverse * scale, (CHUNK, 128))
            flipped[:, rows] = feats[rows, :].T

    project(0, raws[0], own_base)

    def own_step(i, raw, after, base):
        finish(i, raw, own=True)
        project(i + 1, after, base)

    own_step(0, raws[0], raws[1], own_base)
    own_step(1, raws[1], raws[0], other_base)

    def two(j, _):
        finish(2 * j + 2, raws[0])
        project(2 * j + 3, raws[1], other_base)
        finish(2 * j + 3, raws[1])
        project(2 * j + 4, raws[0], other_base)
        return 0

    lax.fori_loop(0, 3, two, 0)
    finish(8, raws[0])
    project(9, raws[1], other_base)
    finish(9, raws[1])

    def score(t, to):
        rows = aligned(BLOCK + t * CHUNK, CHUNK, CHUNK)
        to[...] = rdot(lows[:BLOCK, :], lows[rows, :])

    def weigh(t, came, own=False):
        logits = scale * came[...] + bias
        half = 0.5
        if own:
            r = lax.broadcasted_iota(jnp.int32, logits.shape, 0)
            k = lax.broadcasted_iota(jnp.int32, logits.shape, 1) + t * CHUNK
            half = jnp.where(r == k, -0.5, 0.5)
        share = 0.5 * jnp.tanh(half * logits) + 0.5
        share = 2.0 * half * share if own else share
        weights[:, aligned(t * CHUNK, CHUNK, CHUNK)] = share.astype(bf16)

    score(0, scores[0])
    weigh(0, scores[0], own=True)
    score(1, scores[1])
    weigh(1, scores[1], own=True)
    score(2, scores[0])

    def pair(j, _):
        weigh(2 * j + 2, scores[0])
        score(2 * j + 3, scores[1])
        weigh(2 * j + 3, scores[1])
        score(2 * j + 4, scores[0])
        return 0

    lax.fori_loop(0, 2, pair, 0)
    weigh(6, scores[0])
    score(7, scores[1])
    weigh(7, scores[1])

    def gradient(i, _):
        rows = aligned(i * 192, 192, 192)
        grad = jnp.dot(weights[rows, :], lows[BLOCK:, :], preferred_element_type=f32)
        rounded[rows, :] = before(units, scales, rows, grad)
        return 0

    lax.fori_loop(0, BLOCK // 192, gradient, 0)

    for half in range(2):
        left = slice(half * D // 2, (half + 1) * D // 2)
        for start in range(0, D, 256):
            width = min(256, D - start)
            total = jnp.dot(
                flipped[left, :], rounded[:, start : start + width], preferred_element_type=f32
            )
            for px in range(4):
                for pz in range(4):
                    dx, dz = (px + 4 - x) % 4, (pz + 4 - z) % 4
                    near, far = (dx, dz) if half == 0 else (dz, dx)
                    row = (px * 4 + pz) * SHARE
                    for q in range(width // 128):
                        to = (start // 128 + q) * SHARE
                        staged[half, near, far, to : to + SHARE, :] = total[
                            row : row + SHARE, q * 128 : (q + 1) * 128
                        ]
        for which, out in enumerate((kept, sent)):

            @pl.when(c == (half if which == 0 else 1 - half))
            def _():
                pltpu.make_async_copy(staged.at[half], out, sem_out.at[half]).start()

    for half in range(2):
        pltpu.make_async_copy(staged.at[half], kept, sem_out.at[half]).wait()


def local(at, scalars, pieces, feats):
    anywhere = pl.BlockSpec(memory_space=pl.ANY)
    smem = pl.BlockSpec(memory_space=pltpu.SMEM)
    result = jax.ShapeDtypeStruct((RING, RING, PART, 128), f32)
    return pl.pallas_call(
        local_kernel,
        out_shape=[result, result],
        in_specs=[smem, smem] + [anywhere] * 16,
        out_specs=[anywhere] * 2,
        scratch_shapes=[
            pltpu.VMEM((8, RING, PIECE, 128), bf16),
            pltpu.VMEM((ROWS, D), bf16),
            pltpu.VMEM((D, BLOCK), bf16),
            pltpu.VMEM((2 * D, D), bf16),
            pltpu.VMEM((BLOCK, D), f32),
            pltpu.VMEM((ROWS, D), bf16),
            pltpu.VMEM((BLOCK, 128), f32),
            pltpu.VMEM((BLOCK, OTHERS), bf16),
            pltpu.VMEM((BLOCK, D), bf16),
            pltpu.VMEM((2, RING, RING, PART, 128), f32),
            pltpu.VMEM((CHUNK, D), f32),
            pltpu.VMEM((CHUNK, D), f32),
            pltpu.VMEM((BLOCK, CHUNK), f32),
            pltpu.VMEM((BLOCK, CHUNK), f32),
            pltpu.SemaphoreType.DMA((8,)),
            pltpu.SemaphoreType.DMA((5,)),
            pltpu.SemaphoreType.DMA((4,)),
            pltpu.SemaphoreType.DMA((2,)),
        ],
        compiler_params=pltpu.CompilerParams(vmem_limit_bytes=62 * 2**20),
        cost_estimate=pl.CostEstimate(
            flops=23_100_000_000, bytes_accessed=20_000_000, transcendentals=2_400_000
        ),
        name="local",
    )(at, scalars, *pieces, *feats)


def piece_kernel(at, *refs):
    parts, out, whole = refs[:4], refs[4], refs[5]
    z = at[3]
    for d in range(RING):
        for pz in range(RING):

            @pl.when((z + d) % RING == pz)
            def _():
                whole[pz * SHARE : (pz + 1) * SHARE, :] = parts[d][...].astype(f32)

    for q in range(4):
        out[q * BAND : (q + 1) * BAND, :] = whole[:, q * 128 : (q + 1) * 128].astype(bf16)
    lower = jnp.concatenate(
        [whole[UPPER:, WIDE:], jnp.zeros((2 * UPPER - BAND, 64), f32)], axis=0
    )
    out[4 * BAND :, :] = joined(whole[:UPPER, WIDE:], lower).astype(bf16)


def make_piece(at, parts):
    vmem = pl.BlockSpec(memory_space=pltpu.VMEM)
    return pl.pallas_call(
        piece_kernel,
        out_shape=jax.ShapeDtypeStruct((PIECE, 128), bf16),
        in_specs=[pl.BlockSpec(memory_space=pltpu.SMEM)] + [vmem] * 4,
        out_specs=vmem,
        scratch_shapes=[pltpu.VMEM((BAND, 576), f32)],
        compiler_params=pltpu.CompilerParams(vmem_limit_bytes=8 * 2**20),
        name="make_piece",
    )(at, *parts)


def share_kernel(at, *refs):
    parts, outs = refs[:4], refs[4:]
    c, y = at[0], at[2]
    yl, yh = y % 2, y // 2
    total = parts[0][...] + parts[1][...] + parts[2][...] + parts[3][...]
    for to_core in range(2):
        rows = [
            total[q * SHARE + to_core * 18 : q * SHARE + to_core * 18 + 18, :] for q in range(9)
        ]
        for to_half in range(2):
            tail = rows[8][:, to_half * 64 : to_half * 64 + 64]
            value = jnp.concatenate(rows[4 * to_half : 4 * to_half + 4] + [tail], axis=1)
            for a in range(2):
                for b in range(2):

                    @pl.when((yl == to_core ^ a) & (yh == to_half ^ b))
                    def _():
                        outs[a * 2 + b][...] = value


def make_shares(at, parts):
    vmem = pl.BlockSpec(memory_space=pltpu.VMEM)
    return pl.pallas_call(
        share_kernel,
        out_shape=[jax.ShapeDtypeStruct((18, 576), f32)] * 4,
        in_specs=[pl.BlockSpec(memory_space=pltpu.SMEM)] + [vmem] * 4,
        out_specs=[vmem] * 4,
        compiler_params=pltpu.CompilerParams(vmem_limit_bytes=8 * 2**20),
        name="make_shares",
    )(at, *parts)


def per_device(img_feat, txt_feat, img_head, txt_head, logit_scale, logit_bias):
    yl, x, z, c, yh = (lax.axis_index(a) for a in AXES)
    y = yh * 2 + yl
    at = jnp.stack([c, x, y, z]).astype(jnp.int32)

    first = c == 0
    mine = jnp.where(first, img_head, txt_head)
    come = moved(jnp.where(first, txt_head, img_head), partner)
    rows36 = jnp.where(
        first, jnp.concatenate([mine, come], 0), jnp.concatenate([come, mine], 0)
    )
    parts = [rows36] + [moved(rows36, along_z(-d)) for d in range(1, RING)]
    piece = make_piece(at, parts)

    other_feat = jnp.where(yh == 0, txt_feat, img_feat)
    upper, lower = other_feat[:CHUNK], other_feat[CHUNK:]
    piece, upper, other_feat = lax.optimization_barrier((piece, upper, other_feat))
    upper = moved(upper, mirrored(two_on))
    next_leg = moved(other_feat, mirrored(first_leg))

    near = [piece] + [moved(piece, by_core(along_x(-d), along_y(-d))) for d in range(1, RING)]
    near = jnp.stack(near)
    near, lower = lax.optimization_barrier((near, lower))
    far = [near] + [moved(near, by_core(along_y(-d), along_x(-d))) for d in range(1, RING)]
    lower = moved(lower, mirrored(two_on))
    leg, _ = lax.optimization_barrier((next_leg, near))
    last_leg = moved(leg, mirrored(second_leg))
    other = [moved(a, partner) for a in far]
    upper, lower, _ = lax.optimization_barrier((upper, lower, other))
    halves = [upper, lower, moved(upper, partner), moved(lower, partner)]
    scalars = jnp.concatenate([logit_scale, logit_bias])
    feats = [img_feat, txt_feat, next_leg, last_leg] + halves
    kept, sent = local(at, scalars, far + other, feats)

    come = moved(sent, partner)
    total = kept[0] + come[0]
    for d in range(1, RING):
        share = (kept[d] + come[d]).astype(bf16)
        total = total + moved(share, by_core(along_x(d), along_z(d))).astype(f32)
    parts = [total[0]]
    for d in range(1, RING):
        parts.append(moved(total[d], by_core(along_z(d), along_x(d))))
    shares = make_shares(at, parts)
    results = []
    for b in range(2):
        results.append(moved(shares[b], to_owner(0, b)) + moved(shares[2 + b], to_owner(1, b)))
    return (
        jnp.where(yh == 0, results[0], results[1]),
        jnp.where(yh == 0, results[1], results[0]),
    )


def solution(mesh):
    split = Mesh(mesh.devices.reshape(SIZES), AXES)
    rows, cols = P(DP, None), P(DP, "yh")
    return jax.shard_map(
        per_device,
        mesh=split,
        in_specs=(rows, rows, cols, cols, P(), P()),
        out_specs=(cols, cols),
        check_vma=False,
    )
```

```python
import jax
import jax.numpy as jnp
from jax import lax
from jax.experimental import pallas as pl
from jax.experimental.pallas import tpu as pltpu
from jax.sharding import Mesh
from jax.sharding import PartitionSpec as P


SHIFTS = 4
DP = ("yl", "x", "z", "c")
AXES = ("yl", "x", "z", "c", "yh")
SIZES = (2, 4, 4, 2, 2)
RING = 4
WIDE = 512
D = 1152
BAND = 144
UPPER = 80
PIECE = 656
BLOCK = 768
OTHERS = SHIFTS * BLOCK
ROWS = BLOCK + OTHERS
SHARE = 36
PART = 328
CHUNK = 384

epsilon = 1e-06
f32 = jnp.float32
bf16 = jnp.bfloat16


def place(yl, x, z, c, yh):
    at = 0
    for coordinate, size in zip((yl, x, z, c, yh), SIZES):
        at = at * size + coordinate
    return at


def moved(array, target):
    pairs = []
    for yl in range(2):
        for x in range(4):
            for z in range(4):
                for c in range(2):
                    for yh in range(2):
                        end = target(yl, x, z, c, yh)
                        if end is not None:
                            pairs.append((place(yl, x, z, c, yh), place(*end)))
    return lax.ppermute(array, AXES, pairs)


def along_x(d):
    return lambda yl, x, z, c, yh: (yl, (x + d) % 4, z, c, yh)


def along_y(d):
    def to(yl, x, z, c, yh):
        y = (yh * 2 + yl + d) % 4
        return (y % 2, x, z, c, y // 2)

    return to


def along_z(d):
    return lambda yl, x, z, c, yh: (yl, x, (z + d) % 4, c, yh)


def partner(yl, x, z, c, yh):
    return (yl, x, z, 1 - c, yh)


def by_core(zero, one):
    return lambda yl, x, z, c, yh: (one if c else zero)(yl, x, z, c, yh)


def mirrored(to):
    def both(yl, x, z, c, yh):
        at = (yl, x, z, c) if yh == 0 else (1 - yl, 3 - x, 3 - z, 1 - c)
        end = to(*at)
        if end is None:
            return None
        yl, x, z, c = end if yh == 0 else (1 - end[0], 3 - end[1], 3 - end[2], 1 - end[3])
        return (yl, x, z, c, yh)

    return both


def two_on(yl, x, z, c):
    chip = ((yl * 4 + x) * 4 + z + 1) % 32
    return (chip // 16, chip // 4 % 4, chip % 4, c)


def first_leg(yl, x, z, c):
    return (yl, x, z, 1) if c == 0 else (yl, x, (z - 1) % 4, 0)


def second_leg(yl, x, z, c):
    if c == 1:
        return None
    chip = ((yl * 4 + x) * 4 + (z + 1) % 4 + 2) % 32
    return (chip // 16, chip // 4 % 4, chip % 4, 0)


def to_owner(a, b):
    return lambda yl, x, z, c, yh: (c, x, z, yl ^ a, yh ^ b)


def rdot(left, right):
    return lax.dot_general(left, right, (((1,), (1,)), ((), ())), preferred_element_type=f32)


def position(role, x, y, near, far):
    px = jnp.where(role == 0, (x + near) % 4, (x + far) % 4)
    py = jnp.where(role == 0, (y + far) % 4, (y + near) % 4)
    return px, py


def aligned(start, size, step):
    return pl.ds(pl.multiple_of(start, step), size)


def joined(upper, lower):
    return jnp.concatenate([upper, lower], axis=1)


def before(units, scales, rows, grad):
    unit = units[rows, :]
    inner = jnp.sum(unit * grad, axis=1, keepdims=True)
    return ((grad - unit * inner) * scales[rows, :1]).astype(bf16)


def local_kernel(at, scalars, *refs):
    pieces, (img_in, txt_in, near_in, far_in), halves_in = refs[:8], refs[8:12], refs[12:16]
    kept, sent = refs[16:18]
    held, feats, flipped, heads, units, lows, scales, weights, rounded, staged = refs[18:28]
    raws, scores = refs[28:30], refs[30:32]
    sem_pieces, sem_feats, sem_halves, sem_out = refs[32:]
    c, x, y, z = at[0], at[1], at[2], at[3]
    side = y // 2
    scale, bias = scalars[0], scalars[1]

    loads = [pltpu.make_async_copy(p, held.at[i], sem_pieces.at[i]) for i, p in enumerate(pieces)]
    for copy in loads:
        copy.start()

    def feat_load(i, source):
        return pltpu.make_async_copy(source, feats.at[pl.ds(i * BLOCK, BLOCK)], sem_feats.at[i])

    for copy in loads:
        copy.wait()
    for which, (own, other) in enumerate(((img_in, txt_in), (txt_in, img_in))):

        @pl.when(side == which)
        def _():
            feat_load(0, own).start()
            feat_load(1, other).start()

    half_loads = [
        pltpu.make_async_copy(
            source, feats.at[pl.ds(2 * BLOCK + i * CHUNK, CHUNK)], sem_halves.at[i]
        )
        for i, source in enumerate(halves_in)
    ]
    for copy in half_loads:
        copy.start()
    for which, source in enumerate((far_in, near_in)):

        @pl.when((c + side) % 2 == which)
        def _():
            feat_load(4, source).start()

    def put(i, _):
        source, far, near = i // 16, i // 4 % 4, i % 4
        role = jnp.where(source == 0, c, 1 - c)
        px, py = position(role, x, y, near, far)
        start = role * D + (py % 2 * 4 + px) * BAND
        for half in range(2):

            @pl.when(py // 2 == half)
            def _():
                for q in range(4):
                    cols = slice(half * WIDE + q * 128, half * WIDE + q * 128 + 128)
                    heads[aligned(start, BAND, BAND), cols] = held[
                        source * 4 + far, near, q * BAND : (q + 1) * BAND, :
                    ]
                tail = held[source * 4 + far, near, 4 * BAND :, :]
                cols = slice(2 * WIDE + half * 64, 2 * WIDE + half * 64 + 64)
                heads[aligned(start, UPPER, 16), cols] = tail[:, :64]
                heads[aligned(start + UPPER, BAND - UPPER, 16), cols] = tail[: BAND - UPPER, 64:]

        return 0

    lax.fori_loop(0, 32, put, 0)
    for i in (0, 1, 4):
        feat_load(i, far_in).wait()
    for copy in half_loads:
        copy.wait()

    own_base = pl.multiple_of(side * D, D)
    other_base = pl.multiple_of((1 - side) * D, D)

    def project(i, raw, base):
        rows = aligned(i * CHUNK, CHUNK, CHUNK)
        for start in range(0, D, 256):
            width = min(256, D - start)
            cols = slice(start, start + width)
            raw[:, cols] = jnp.dot(
                feats[rows, :], heads[pl.ds(base, D), cols], preferred_element_type=f32
            )

    def finish(i, raw, own=False):
        rows = aligned(i * CHUNK, CHUNK, CHUNK)
        proj = raw[...]
        square = jnp.sum(proj * proj, axis=1, keepdims=True)
        inverse = 1.0 / jnp.sqrt(square + epsilon)
        unit = proj * inverse
        lows[rows, :] = unit.astype(bf16)
        if own:
            units[rows, :] = unit
            scales[rows, :] = jnp.broadcast_to(inverse * scale, (CHUNK, 128))
            flipped[:, rows] = feats[rows, :].T

    project(0, raws[0], own_base)

    def own_step(i, raw, after, base):
        finish(i, raw, own=True)
        project(i + 1, after, base)

    own_step(0, raws[0], raws[1], own_base)
    own_step(1, raws[1], raws[0], other_base)

    def two(j, _):
        finish(2 * j + 2, raws[0])
        project(2 * j + 3, raws[1], other_base)
        finish(2 * j + 3, raws[1])
        project(2 * j + 4, raws[0], other_base)
        return 0

    lax.fori_loop(0, 3, two, 0)
    finish(8, raws[0])
    project(9, raws[1], other_base)
    finish(9, raws[1])

    def score(t, to):
        rows = aligned(BLOCK + t * CHUNK, CHUNK, CHUNK)
        to[...] = rdot(lows[:BLOCK, :], lows[rows, :])

    def weigh(t, came, own=False):
        logits = scale * came[...] + bias
        half = 0.5
        if own:
            r = lax.broadcasted_iota(jnp.int32, logits.shape, 0)
            k = lax.broadcasted_iota(jnp.int32, logits.shape, 1) + t * CHUNK
            half = jnp.where(r == k, -0.5, 0.5)
        share = 0.5 * jnp.tanh(half * logits) + 0.5
        share = 2.0 * half * share if own else share
        weights[:, aligned(t * CHUNK, CHUNK, CHUNK)] = share.astype(bf16)

    score(0, scores[0])
    weigh(0, scores[0], own=True)
    score(1, scores[1])
    weigh(1, scores[1], own=True)
    score(2, scores[0])

    def pair(j, _):
        weigh(2 * j + 2, scores[0])
        score(2 * j + 3, scores[1])
        weigh(2 * j + 3, scores[1])
        score(2 * j + 4, scores[0])
        return 0

    lax.fori_loop(0, 2, pair, 0)
    weigh(6, scores[0])
    score(7, scores[1])
    weigh(7, scores[1])

    def gradient(i, _):
        rows = aligned(i * 192, 192, 192)
        grad = jnp.dot(weights[rows, :], lows[BLOCK:, :], preferred_element_type=f32)
        rounded[rows, :] = before(units, scales, rows, grad)
        return 0

    lax.fori_loop(0, BLOCK // 192, gradient, 0)

    for half in range(2):
        left = slice(half * D // 2, (half + 1) * D // 2)
        for start in range(0, D, 256):
            width = min(256, D - start)
            total = jnp.dot(
                flipped[left, :], rounded[:, start : start + width], preferred_element_type=f32
            )
            for px in range(4):
                for pz in range(4):
                    dx, dz = (px + 4 - x) % 4, (pz + 4 - z) % 4
                    near, far = (dx, dz) if half == 0 else (dz, dx)
                    row = (px * 4 + pz) * SHARE
                    for q in range(width // 128):
                        to = (start // 128 + q) * SHARE
                        staged[half, near, far, to : to + SHARE, :] = total[
                            row : row + SHARE, q * 128 : (q + 1) * 128
                        ]
        for which, out in enumerate((kept, sent)):

            @pl.when(c == (half if which == 0 else 1 - half))
            def _():
                pltpu.make_async_copy(staged.at[half], out, sem_out.at[half]).start()

    for half in range(2):
        pltpu.make_async_copy(staged.at[half], kept, sem_out.at[half]).wait()


def local(at, scalars, pieces, feats):
    anywhere = pl.BlockSpec(memory_space=pl.ANY)
    smem = pl.BlockSpec(memory_space=pltpu.SMEM)
    result = jax.ShapeDtypeStruct((RING, RING, PART, 128), f32)
    return pl.pallas_call(
        local_kernel,
        out_shape=[result, result],
        in_specs=[smem, smem] + [anywhere] * 16,
        out_specs=[anywhere] * 2,
        scratch_shapes=[
            pltpu.VMEM((8, RING, PIECE, 128), bf16),
            pltpu.VMEM((ROWS, D), bf16),
            pltpu.VMEM((D, BLOCK), bf16),
            pltpu.VMEM((2 * D, D), bf16),
            pltpu.VMEM((BLOCK, D), f32),
            pltpu.VMEM((ROWS, D), bf16),
            pltpu.VMEM((BLOCK, 128), f32),
            pltpu.VMEM((BLOCK, OTHERS), bf16),
            pltpu.VMEM((BLOCK, D), bf16),
            pltpu.VMEM((2, RING, RING, PART, 128), f32),
            pltpu.VMEM((CHUNK, D), f32),
            pltpu.VMEM((CHUNK, D), f32),
            pltpu.VMEM((BLOCK, CHUNK), f32),
            pltpu.VMEM((BLOCK, CHUNK), f32),
            pltpu.SemaphoreType.DMA((8,)),
            pltpu.SemaphoreType.DMA((5,)),
            pltpu.SemaphoreType.DMA((4,)),
            pltpu.SemaphoreType.DMA((2,)),
        ],
        compiler_params=pltpu.CompilerParams(vmem_limit_bytes=62 * 2**20),
        cost_estimate=pl.CostEstimate(
            flops=23_100_000_000, bytes_accessed=20_000_000, transcendentals=2_400_000
        ),
        name="local",
    )(at, scalars, *pieces, *feats)


def piece_kernel(at, *refs):
    parts, out, whole = refs[:4], refs[4], refs[5]
    z = at[3]
    for d in range(RING):
        for pz in range(RING):

            @pl.when((z + d) % RING == pz)
            def _():
                whole[pz * SHARE : (pz + 1) * SHARE, :] = parts[d][...].astype(f32)

    for q in range(4):
        out[q * BAND : (q + 1) * BAND, :] = whole[:, q * 128 : (q + 1) * 128].astype(bf16)
    lower = jnp.concatenate(
        [whole[UPPER:, WIDE:], jnp.zeros((2 * UPPER - BAND, 64), f32)], axis=0
    )
    out[4 * BAND :, :] = joined(whole[:UPPER, WIDE:], lower).astype(bf16)


def make_piece(at, parts):
    vmem = pl.BlockSpec(memory_space=pltpu.VMEM)
    return pl.pallas_call(
        piece_kernel,
        out_shape=jax.ShapeDtypeStruct((PIECE, 128), bf16),
        in_specs=[pl.BlockSpec(memory_space=pltpu.SMEM)] + [vmem] * 4,
        out_specs=vmem,
        scratch_shapes=[pltpu.VMEM((BAND, 576), f32)],
        compiler_params=pltpu.CompilerParams(vmem_limit_bytes=8 * 2**20),
        name="make_piece",
    )(at, *parts)


def share_kernel(at, *refs):
    parts, outs = refs[:4], refs[4:]
    y = at[2]
    yl, yh = y % 2, y // 2
    total = parts[0][...] + parts[1][...] + parts[2][...] + parts[3][...]
    for to_core in range(2):
        rows = [
            total[q * SHARE + to_core * 18 : q * SHARE + to_core * 18 + 18, :] for q in range(9)
        ]
        for to_half in range(2):
            tail = rows[8][:, to_half * 64 : to_half * 64 + 64]
            value = jnp.concatenate(rows[4 * to_half : 4 * to_half + 4] + [tail], axis=1)
            for a in range(2):
                for b in range(2):

                    @pl.when((yl == to_core ^ a) & (yh == to_half ^ b))
                    def _():
                        outs[a * 2 + b][...] = value


def make_shares(at, parts):
    vmem = pl.BlockSpec(memory_space=pltpu.VMEM)
    return pl.pallas_call(
        share_kernel,
        out_shape=[jax.ShapeDtypeStruct((18, 576), f32)] * 4,
        in_specs=[pl.BlockSpec(memory_space=pltpu.SMEM)] + [vmem] * 4,
        out_specs=[vmem] * 4,
        compiler_params=pltpu.CompilerParams(vmem_limit_bytes=8 * 2**20),
        name="make_shares",
    )(at, *parts)


def gradients(img_feat, txt_feat, img_head, txt_head, logit_scale, logit_bias):
    yl, x, z, c, yh = (lax.axis_index(a) for a in AXES)
    y = yh * 2 + yl
    at = jnp.stack([c, x, y, z]).astype(jnp.int32)

    first = c == 0
    mine = jnp.where(first, img_head, txt_head)
    come = moved(jnp.where(first, txt_head, img_head), partner)
    rows36 = jnp.where(
        first, jnp.concatenate([mine, come], 0), jnp.concatenate([come, mine], 0)
    )
    parts = [rows36] + [moved(rows36, along_z(-d)) for d in range(1, RING)]
    piece = make_piece(at, parts)

    other_feat = jnp.where(yh == 0, txt_feat, img_feat)
    upper, lower = other_feat[:CHUNK], other_feat[CHUNK:]
    piece, upper, other_feat = lax.optimization_barrier((piece, upper, other_feat))
    upper = moved(upper, mirrored(two_on))
    next_leg = moved(other_feat, mirrored(first_leg))

    near = [piece]
    for d in range(1, RING):
        near.append(moved(piece, by_core(along_x(-d), along_y(-d))))
    near = jnp.stack(near)
    near, lower = lax.optimization_barrier((near, lower))
    far = [near]
    for d in range(1, RING):
        far.append(moved(near, by_core(along_y(-d), along_x(-d))))
    lower = moved(lower, mirrored(two_on))
    leg, _ = lax.optimization_barrier((next_leg, near))
    last_leg = moved(leg, mirrored(second_leg))
    other = [moved(a, partner) for a in far]
    upper, lower, _ = lax.optimization_barrier((upper, lower, other))
    halves = [upper, lower, moved(upper, partner), moved(lower, partner)]
    scalars = jnp.concatenate([logit_scale, logit_bias])
    feats = [img_feat, txt_feat, next_leg, last_leg] + halves
    kept, sent = local(at, scalars, far + other, feats)

    come = moved(sent, partner)
    total = kept[0] + come[0]
    for d in range(1, RING):
        share = (kept[d] + come[d]).astype(bf16)
        total = total + moved(share, by_core(along_x(d), along_z(d))).astype(f32)
    parts = [total[0]]
    for d in range(1, RING):
        parts.append(moved(total[d], by_core(along_z(d), along_x(d))))
    shares = make_shares(at, parts)
    results = []
    for b in range(2):
        results.append(moved(shares[b], to_owner(0, b)) + moved(shares[2 + b], to_owner(1, b)))
    return (
        jnp.where(yh == 0, results[0], results[1]),
        jnp.where(yh == 0, results[1], results[0]),
    )


def solution(mesh):
    split = Mesh(mesh.devices.reshape(SIZES), AXES)
    rows, cols = P(DP, None), P(DP, "yh")
    return jax.shard_map(
        gradients,
        mesh=split,
        in_specs=(rows, rows, cols, cols, P(), P()),
        out_specs=(cols, cols),
        check_vma=False,
    )
```

```python
import jax
import jax.numpy as jnp
from jax import lax
from jax.experimental import pallas as pl
from jax.experimental.pallas import tpu as pltpu
from jax.sharding import Mesh
from jax.sharding import PartitionSpec as P

SHIFTS = 4
DP = ("yl", "x", "z", "c")
AXES = ("yl", "x", "z", "c", "yh")
SIZES = (2, 4, 4, 2, 2)
RING = 4
WIDE = 512
D = 1152
BAND = 144
UPPER = 80
PIECE = 656
BLOCK = 768
OTHERS = SHIFTS * BLOCK
ROWS = BLOCK + OTHERS
SHARE = 36
PART = 328
CHUNK = 384

epsilon = 1e-06
f32 = jnp.float32
bf16 = jnp.bfloat16


def place(yl, x, z, c, yh):
    at = 0
    for coordinate, size in zip((yl, x, z, c, yh), SIZES):
        at = at * size + coordinate
    return at


def moved(array, target):
    pairs = []
    for yl in range(2):
        for x in range(4):
            for z in range(4):
                for c in range(2):
                    for yh in range(2):
                        end = target(yl, x, z, c, yh)
                        if end is not None:
                            pairs.append((place(yl, x, z, c, yh), place(*end)))
    return lax.ppermute(array, AXES, pairs)


def along_x(d):
    return lambda yl, x, z, c, yh: (yl, (x + d) % 4, z, c, yh)


def along_y(d):
    def to(yl, x, z, c, yh):
        y = (yh * 2 + yl + d) % 4
        return (y % 2, x, z, c, y // 2)

    return to


def along_z(d):
    return lambda yl, x, z, c, yh: (yl, x, (z + d) % 4, c, yh)


def partner(yl, x, z, c, yh):
    return (yl, x, z, 1 - c, yh)


def by_core(zero, one):
    return lambda yl, x, z, c, yh: (one if c else zero)(yl, x, z, c, yh)


def mirrored(to):
    def both(yl, x, z, c, yh):
        at = (yl, x, z, c) if yh == 0 else (1 - yl, 3 - x, 3 - z, 1 - c)
        end = to(*at)
        if end is None:
            return None
        yl, x, z, c = end if yh == 0 else (1 - end[0], 3 - end[1], 3 - end[2], 1 - end[3])
        return (yl, x, z, c, yh)

    return both


def two_on(yl, x, z, c):
    chip = ((yl * 4 + x) * 4 + z + 1) % 32
    return (chip // 16, chip // 4 % 4, chip % 4, c)


def first_leg(yl, x, z, c):
    return (yl, x, z, 1) if c == 0 else (yl, x, (z - 1) % 4, 0)


def second_leg(yl, x, z, c):
    if c == 1:
        return None
    chip = ((yl * 4 + x) * 4 + (z + 1) % 4 + 2) % 32
    return (chip // 16, chip // 4 % 4, chip % 4, 0)


def to_owner(a, b):
    return lambda yl, x, z, c, yh: (c, x, z, yl ^ a, yh ^ b)


def tdot(left, right):
    return lax.dot_general(left, right, (((0,), (0,)), ((), ())), preferred_element_type=f32)


def rdot(left, right):
    return lax.dot_general(left, right, (((1,), (1,)), ((), ())), preferred_element_type=f32)


def position(role, x, y, near, far):
    px = jnp.where(role == 0, (x + near) % 4, (x + far) % 4)
    py = jnp.where(role == 0, (y + far) % 4, (y + near) % 4)
    return px, py


def aligned(start, size, step):
    return pl.ds(pl.multiple_of(start, step), size)


def joined(upper, lower):
    return jnp.concatenate([upper, lower], axis=1)


def before(units, scales, rows, grad):
    unit = units[rows, :]
    inner = jnp.sum(unit * grad, axis=1, keepdims=True)
    return ((grad - unit * inner) * scales[rows, :1]).astype(bf16)


def first_kernel(at, scalars, *refs):
    pieces, (img_in, txt_in) = refs[:8], refs[8:10]
    outs = refs[10:15]
    held, feats, flipped, heads, units, lows, scales = refs[15:22]
    raws = refs[22:24]
    sem_pieces, sem_feats, sem_out = refs[24:]
    c, x, y = at[0], at[1], at[2]
    side = y // 2
    scale = scalars[0]

    loads = [pltpu.make_async_copy(p, held.at[i], sem_pieces.at[i]) for i, p in enumerate(pieces)]
    for copy in loads:
        copy.start()

    def feat_load(i, source):
        return pltpu.make_async_copy(source, feats.at[pl.ds(i * BLOCK, BLOCK)], sem_feats.at[i])

    for copy in loads:
        copy.wait()
    for which, (own, other) in enumerate(((img_in, txt_in), (txt_in, img_in))):

        @pl.when(side == which)
        def _():
            feat_load(0, own).start()
            feat_load(1, other).start()

    def put(i, _):
        source, far, near = i // 16, i // 4 % 4, i % 4
        role = jnp.where(source == 0, c, 1 - c)
        px, py = position(role, x, y, near, far)
        start = role * D + (py % 2 * 4 + px) * BAND
        for half in range(2):

            @pl.when(py // 2 == half)
            def _():
                for q in range(4):
                    cols = slice(half * WIDE + q * 128, half * WIDE + q * 128 + 128)
                    heads[aligned(start, BAND, BAND), cols] = held[
                        source * 4 + far, near, q * BAND : (q + 1) * BAND, :
                    ]
                tail = held[source * 4 + far, near, 4 * BAND :, :]
                cols = slice(2 * WIDE + half * 64, 2 * WIDE + half * 64 + 64)
                heads[aligned(start, UPPER, 16), cols] = tail[:, :64]
                heads[aligned(start + UPPER, BAND - UPPER, 16), cols] = tail[: BAND - UPPER, 64:]

        return 0

    lax.fori_loop(0, 32, put, 0)
    for i in range(2):
        feat_load(i, img_in).wait()

    own_base = pl.multiple_of(side * D, D)
    other_base = pl.multiple_of((1 - side) * D, D)

    def project(i, raw, base):
        rows = aligned(i * CHUNK, CHUNK, CHUNK)
        for start in range(0, D, 256):
            width = min(256, D - start)
            cols = slice(start, start + width)
            raw[:, cols] = jnp.dot(
                feats[rows, :], heads[pl.ds(base, D), cols], preferred_element_type=f32
            )

    def finish(i, raw, own=False):
        rows = aligned(i * CHUNK, CHUNK, CHUNK)
        proj = raw[...]
        square = jnp.sum(proj * proj, axis=1, keepdims=True)
        inverse = 1.0 / jnp.sqrt(square + epsilon)
        unit = proj * inverse
        lows[rows, :] = unit.astype(bf16)
        if own:
            units[rows, :] = unit
            scales[rows, :] = jnp.broadcast_to(inverse * scale, (CHUNK, 128))
            flipped[:, rows] = feats[rows, :].T

    other_heads = heads.at[pl.ds(other_base, D)]
    stores = [
        pltpu.make_async_copy(ref, out, sem_out.at[i])
        for i, (ref, out) in enumerate(zip((other_heads, units, lows, flipped, scales), outs))
    ]
    stores[0].start()
    project(0, raws[0], own_base)
    finish(0, raws[0], own=True)
    project(1, raws[1], own_base)
    finish(1, raws[1], own=True)
    for i in (1, 3, 4):
        stores[i].start()
    project(2, raws[0], other_base)
    finish(2, raws[0])
    project(3, raws[1], other_base)
    finish(3, raws[1])
    stores[2].start()
    for copy in stores:
        copy.wait()


def second_kernel(at, scalars, *refs):
    heads_in, units_in, lows_in, flipped_in, scales_in = refs[:5]
    near_in, far_in = refs[5:7]
    halves_in = refs[7:11]
    kept, sent = refs[11:13]
    feats, flipped, heads, units, lows, scales, weights, rounded, staged = refs[13:22]
    raws, scores = refs[22:24], refs[24:26]
    sem_kept, sem_last, sem_halves, sem_out = refs[26:]
    c, x, y, z = at[0], at[1], at[2], at[3]
    side = y // 2
    scale, bias = scalars[0], scalars[1]
    half_loads = [
        pltpu.make_async_copy(source, feats.at[pl.ds(i * CHUNK, CHUNK)], sem_halves.at[i])
        for i, source in enumerate(halves_in)
    ]

    def last_load(source):
        return pltpu.make_async_copy(source, feats.at[pl.ds(2 * BLOCK, BLOCK)], sem_last.at[0])

    kept_loads = [
        pltpu.make_async_copy(source, to, sem_kept.at[i])
        for i, (source, to) in enumerate(
            (
                (heads_in, heads),
                (units_in, units),
                (lows_in, lows.at[pl.ds(0, 2 * BLOCK)]),
                (flipped_in, flipped),
                (scales_in, scales),
            )
        )
    ]
    kept_loads[0].start()
    for copy in half_loads:
        copy.start()
    for which, source in enumerate((far_in, near_in)):

        @pl.when((c + side) % 2 == which)
        def _():
            last_load(source).start()

    kept_loads[0].wait()
    for copy in half_loads:
        copy.wait()
    for copy in kept_loads[1:]:
        copy.start()

    def project(i, raw):
        rows = aligned(i * CHUNK, CHUNK, CHUNK)
        for start in range(0, D, 256):
            width = min(256, D - start)
            cols = slice(start, start + width)
            raw[:, cols] = jnp.dot(feats[rows, :], heads[:, cols], preferred_element_type=f32)

    def finish(i, raw):
        rows = aligned(2 * BLOCK + i * CHUNK, CHUNK, CHUNK)
        proj = raw[...]
        square = jnp.sum(proj * proj, axis=1, keepdims=True)
        lows[rows, :] = (proj * (1.0 / jnp.sqrt(square + epsilon))).astype(bf16)

    project(0, raws[0])

    def two(j, _):
        finish(2 * j, raws[0])
        project(2 * j + 1, raws[1])
        finish(2 * j + 1, raws[1])
        project(2 * j + 2, raws[0])
        return 0

    lax.fori_loop(0, 1, two, 0)
    last_load(far_in).wait()
    lax.fori_loop(1, 2, two, 0)
    finish(4, raws[0])
    project(5, raws[1])
    finish(5, raws[1])
    for copy in kept_loads[1:]:
        copy.wait()

    def score(t, to):
        rows = aligned(BLOCK + t * CHUNK, CHUNK, CHUNK)
        to[...] = rdot(lows[:BLOCK, :], lows[rows, :])

    def weigh(t, came, own=False):
        logits = scale * came[...] + bias
        half = 0.5
        if own:
            r = lax.broadcasted_iota(jnp.int32, logits.shape, 0)
            k = lax.broadcasted_iota(jnp.int32, logits.shape, 1) + t * CHUNK
            half = jnp.where(r == k, -0.5, 0.5)
        share = 0.5 * jnp.tanh(half * logits) + 0.5
        share = 2.0 * half * share if own else share
        weights[:, aligned(t * CHUNK, CHUNK, CHUNK)] = share.astype(bf16)

    score(0, scores[0])
    weigh(0, scores[0], own=True)
    score(1, scores[1])
    weigh(1, scores[1], own=True)
    score(2, scores[0])

    def pair(j, _):
        weigh(2 * j + 2, scores[0])
        score(2 * j + 3, scores[1])
        weigh(2 * j + 3, scores[1])
        score(2 * j + 4, scores[0])
        return 0

    lax.fori_loop(0, 2, pair, 0)
    weigh(6, scores[0])
    score(7, scores[1])
    weigh(7, scores[1])

    def gradient(i, _):
        rows = aligned(i * 192, 192, 192)
        grad = jnp.dot(weights[rows, :], lows[BLOCK:, :], preferred_element_type=f32)
        rounded[rows, :] = before(units, scales, rows, grad)
        return 0

    lax.fori_loop(0, BLOCK // 192, gradient, 0)

    for half in range(2):
        left = slice(half * D // 2, (half + 1) * D // 2)
        for start in range(0, D, 256):
            width = min(256, D - start)
            total = jnp.dot(
                flipped[left, :], rounded[:, start : start + width], preferred_element_type=f32
            )
            for px in range(4):
                for pz in range(4):
                    dx, dz = (px + 4 - x) % 4, (pz + 4 - z) % 4
                    near, far = (dx, dz) if half == 0 else (dz, dx)
                    row = (px * 4 + pz) * SHARE
                    for q in range(width // 128):
                        to = (start // 128 + q) * SHARE
                        staged[half, near, far, to : to + SHARE, :] = total[
                            row : row + SHARE, q * 128 : (q + 1) * 128
                        ]
        for which, out in enumerate((kept, sent)):

            @pl.when(c == (half if which == 0 else 1 - half))
            def _():
                pltpu.make_async_copy(staged.at[half], out, sem_out.at[half]).start()

    for half in range(2):
        pltpu.make_async_copy(staged.at[half], kept, sem_out.at[half]).wait()


def scratch(shape, kind=bf16):
    return pltpu.VMEM(shape, kind)


def first(at, scalars, pieces, feats):
    anywhere = pl.BlockSpec(memory_space=pl.ANY)
    smem = pl.BlockSpec(memory_space=pltpu.SMEM)
    shape = jax.ShapeDtypeStruct
    return pl.pallas_call(
        first_kernel,
        out_shape=[
            shape((D, D), bf16),
            shape((BLOCK, D), f32),
            shape((2 * BLOCK, D), bf16),
            shape((D, BLOCK), bf16),
            shape((BLOCK, 128), f32),
        ],
        in_specs=[smem, smem] + [anywhere] * 10,
        out_specs=[anywhere] * 5,
        scratch_shapes=[
            scratch((8, RING, PIECE, 128)),
            scratch((2 * BLOCK, D)),
            scratch((D, BLOCK)),
            scratch((2 * D, D)),
            scratch((BLOCK, D), f32),
            scratch((2 * BLOCK, D)),
            scratch((BLOCK, 128), f32),
            scratch((CHUNK, D), f32),
            scratch((CHUNK, D), f32),
            pltpu.SemaphoreType.DMA((8,)),
            pltpu.SemaphoreType.DMA((2,)),
            pltpu.SemaphoreType.DMA((5,)),
        ],
        compiler_params=pltpu.CompilerParams(vmem_limit_bytes=60 * 2**20),
        cost_estimate=pl.CostEstimate(
            flops=4_100_000_000, bytes_accessed=20_000_000, transcendentals=0
        ),
        name="first",
    )(at, scalars, *pieces, *feats)


def second(at, scalars, held, feats):
    anywhere = pl.BlockSpec(memory_space=pl.ANY)
    smem = pl.BlockSpec(memory_space=pltpu.SMEM)
    result = jax.ShapeDtypeStruct((RING, RING, PART, 128), f32)
    return pl.pallas_call(
        second_kernel,
        out_shape=[result, result],
        in_specs=[smem, smem] + [anywhere] * 11,
        out_specs=[anywhere] * 2,
        scratch_shapes=[
            scratch((3 * BLOCK, D)),
            scratch((D, BLOCK)),
            scratch((D, D)),
            scratch((BLOCK, D), f32),
            scratch((ROWS, D)),
            scratch((BLOCK, 128), f32),
            scratch((BLOCK, OTHERS)),
            scratch((BLOCK, D)),
            scratch((2, RING, RING, PART, 128), f32),
            scratch((CHUNK, D), f32),
            scratch((CHUNK, D), f32),
            scratch((BLOCK, CHUNK), f32),
            scratch((BLOCK, CHUNK), f32),
            pltpu.SemaphoreType.DMA((5,)),
            pltpu.SemaphoreType.DMA((1,)),
            pltpu.SemaphoreType.DMA((4,)),
            pltpu.SemaphoreType.DMA((2,)),
        ],
        compiler_params=pltpu.CompilerParams(vmem_limit_bytes=60 * 2**20),
        cost_estimate=pl.CostEstimate(
            flops=19_000_000_000, bytes_accessed=22_000_000, transcendentals=2_400_000
        ),
        name="second",
    )(at, scalars, *held, *feats)


def piece_kernel(at, *refs):
    parts, out, whole = refs[:4], refs[4], refs[5]
    z = at[3]
    for d in range(RING):
        for pz in range(RING):

            @pl.when((z + d) % RING == pz)
            def _():
                whole[pz * SHARE : (pz + 1) * SHARE, :] = parts[d][...].astype(f32)

    for q in range(4):
        out[q * BAND : (q + 1) * BAND, :] = whole[:, q * 128 : (q + 1) * 128].astype(bf16)
    lower = jnp.concatenate(
        [whole[UPPER:, WIDE:], jnp.zeros((2 * UPPER - BAND, 64), f32)], axis=0
    )
    out[4 * BAND :, :] = joined(whole[:UPPER, WIDE:], lower).astype(bf16)


def make_piece(at, parts):
    vmem = pl.BlockSpec(memory_space=pltpu.VMEM)
    return pl.pallas_call(
        piece_kernel,
        out_shape=jax.ShapeDtypeStruct((PIECE, 128), bf16),
        in_specs=[pl.BlockSpec(memory_space=pltpu.SMEM)] + [vmem] * 4,
        out_specs=vmem,
        scratch_shapes=[pltpu.VMEM((BAND, 576), f32)],
        compiler_params=pltpu.CompilerParams(vmem_limit_bytes=8 * 2**20),
        name="make_piece",
    )(at, *parts)


def share_kernel(at, *refs):
    parts, outs = refs[:4], refs[4:]
    c, y = at[0], at[2]
    yl, yh = y % 2, y // 2
    total = parts[0][...] + parts[1][...] + parts[2][...] + parts[3][...]
    for to_core in range(2):
        rows = [
            total[q * SHARE + to_core * 18 : q * SHARE + to_core * 18 + 18, :] for q in range(9)
        ]
        for to_half in range(2):
            tail = rows[8][:, to_half * 64 : to_half * 64 + 64]
            value = jnp.concatenate(rows[4 * to_half : 4 * to_half + 4] + [tail], axis=1)
            for a in range(2):
                for b in range(2):

                    @pl.when((yl == to_core ^ a) & (yh == to_half ^ b))
                    def _():
                        outs[a * 2 + b][...] = value


def make_shares(at, parts):
    vmem = pl.BlockSpec(memory_space=pltpu.VMEM)
    return pl.pallas_call(
        share_kernel,
        out_shape=[jax.ShapeDtypeStruct((18, 576), f32)] * 4,
        in_specs=[pl.BlockSpec(memory_space=pltpu.SMEM)] + [vmem] * 4,
        out_specs=[vmem] * 4,
        compiler_params=pltpu.CompilerParams(vmem_limit_bytes=8 * 2**20),
        name="make_shares",
    )(at, *parts)


def per_device(img_feat, txt_feat, img_head, txt_head, logit_scale, logit_bias):
    yl, x, z, c, yh = (lax.axis_index(a) for a in AXES)
    y = yh * 2 + yl
    at = jnp.stack([c, x, y, z]).astype(jnp.int32)

    is_first = c == 0
    mine = jnp.where(is_first, img_head, txt_head)
    come = moved(jnp.where(is_first, txt_head, img_head), partner)
    rows36 = jnp.where(
        is_first, jnp.concatenate([mine, come], 0), jnp.concatenate([come, mine], 0)
    )
    parts = [rows36] + [moved(rows36, along_z(-d)) for d in range(1, RING)]
    piece = make_piece(at, parts)

    other_feat = jnp.where(yh == 0, txt_feat, img_feat)
    upper, lower = other_feat[:CHUNK], other_feat[CHUNK:]
    piece, other_feat = lax.optimization_barrier((piece, other_feat))
    next_leg = moved(other_feat, mirrored(first_leg))

    near = [piece] + [moved(piece, by_core(along_x(-d), along_y(-d))) for d in range(1, RING)]
    near = jnp.stack(near)
    far = [near] + [moved(near, by_core(along_y(-d), along_x(-d))) for d in range(1, RING)]
    leg, upper, lower, _ = lax.optimization_barrier((next_leg, upper, lower, far))
    upper = moved(upper, mirrored(two_on))
    lower = moved(lower, mirrored(two_on))
    last_leg = moved(leg, mirrored(second_leg))
    other = [moved(a, partner) for a in far]
    scalars = jnp.concatenate([logit_scale, logit_bias])
    held = first(at, scalars, far + other, [img_feat, txt_feat])
    upper, lower, held = lax.optimization_barrier((upper, lower, held))
    halves = [upper, lower, moved(upper, partner), moved(lower, partner)]
    kept, sent = second(at, scalars, held, [next_leg, last_leg] + halves)

    come = moved(sent, partner)
    total = kept[0] + come[0]
    for d in range(1, RING):
        share = (kept[d] + come[d]).astype(bf16)
        total = total + moved(share, by_core(along_x(d), along_z(d))).astype(f32)
    parts = [total[0]]
    for d in range(1, RING):
        parts.append(moved(total[d], by_core(along_z(d), along_x(d))))
    shares = make_shares(at, parts)
    results = []
    for b in range(2):
        results.append(moved(shares[b], to_owner(0, b)) + moved(shares[2 + b], to_owner(1, b)))
    return (
        jnp.where(yh == 0, results[0], results[1]),
        jnp.where(yh == 0, results[1], results[0]),
    )


def solution(mesh):
    split = Mesh(mesh.devices.reshape(SIZES), AXES)
    rows, cols = P(DP, None), P(DP, "yh")
    return jax.shard_map(
        per_device,
        mesh=split,
        in_specs=(rows, rows, cols, cols, P(), P()),
        out_specs=(cols, cols),
        check_vma=False,
    )
```

```python
import jax
import jax.numpy as jnp
from jax import lax
from jax.experimental import pallas as pl
from jax.experimental.pallas import tpu as pltpu
from jax.sharding import Mesh
from jax.sharding import PartitionSpec as P

SHIFTS = 4
DP = ("yl", "x", "z", "c")
AXES = ("yl", "x", "z", "c", "yh")
SIZES = (2, 4, 4, 2, 2)
RING = 4
WIDE = 512
D = 1152
BAND = 144
UPPER = 80
PIECE = 656
BLOCK = 768
OTHERS = SHIFTS * BLOCK
ROWS = BLOCK + OTHERS
SHARE = 36
PART = 328
CHUNK = 384

epsilon = 1e-06
f32 = jnp.float32
bf16 = jnp.bfloat16


def place(yl, x, z, c, yh):
    at = 0
    for coordinate, size in zip((yl, x, z, c, yh), SIZES):
        at = at * size + coordinate
    return at


def moved(array, target):
    pairs = []
    for yl in range(2):
        for x in range(4):
            for z in range(4):
                for c in range(2):
                    for yh in range(2):
                        end = target(yl, x, z, c, yh)
                        if end is not None:
                            pairs.append((place(yl, x, z, c, yh), place(*end)))
    return lax.ppermute(array, AXES, pairs)


def along_x(d):
    return lambda yl, x, z, c, yh: (yl, (x + d) % 4, z, c, yh)


def along_y(d):
    def to(yl, x, z, c, yh):
        y = (yh * 2 + yl + d) % 4
        return (y % 2, x, z, c, y // 2)

    return to


def along_z(d):
    return lambda yl, x, z, c, yh: (yl, x, (z + d) % 4, c, yh)


def partner(yl, x, z, c, yh):
    return (yl, x, z, 1 - c, yh)


def by_core(zero, one):
    return lambda yl, x, z, c, yh: (one if c else zero)(yl, x, z, c, yh)


def mirrored(to):
    def both(yl, x, z, c, yh):
        at = (yl, x, z, c) if yh == 0 else (1 - yl, 3 - x, 3 - z, 1 - c)
        end = to(*at)
        if end is None:
            return None
        yl, x, z, c = end if yh == 0 else (1 - end[0], 3 - end[1], 3 - end[2], 1 - end[3])
        return (yl, x, z, c, yh)

    return both


def two_on(yl, x, z, c):
    chip = ((yl * 4 + x) * 4 + z + 1) % 32
    return (chip // 16, chip // 4 % 4, chip % 4, c)


def first_leg(yl, x, z, c):
    return (yl, x, z, 1) if c == 0 else (yl, x, (z - 1) % 4, 0)


def second_leg(yl, x, z, c):
    if c == 1:
        return None
    chip = ((yl * 4 + x) * 4 + (z + 1) % 4 + 2) % 32
    return (chip // 16, chip // 4 % 4, chip % 4, 0)


def to_owner(a, b):
    return lambda yl, x, z, c, yh: (c, x, z, yl ^ a, yh ^ b)


def tdot(left, right):
    return lax.dot_general(left, right, (((0,), (0,)), ((), ())), preferred_element_type=f32)


def rdot(left, right):
    return lax.dot_general(left, right, (((1,), (1,)), ((), ())), preferred_element_type=f32)


def position(role, x, y, near, far):
    px = jnp.where(role == 0, (x + near) % 4, (x + far) % 4)
    py = jnp.where(role == 0, (y + far) % 4, (y + near) % 4)
    return px, py


def aligned(start, size, step):
    return pl.ds(pl.multiple_of(start, step), size)


def joined(upper, lower):
    return jnp.concatenate([upper, lower], axis=1)


def before(units, scales, rows, grad):
    unit = units[rows, :]
    inner = jnp.sum(unit * grad, axis=1, keepdims=True)
    return ((grad - unit * inner) * scales[rows, :1]).astype(bf16)


def first_kernel(at, scalars, *refs):
    pieces, (img_in, txt_in) = refs[:8], refs[8:10]
    outs = refs[10:15]
    held, feats, flipped, heads, units, lows, scales = refs[15:22]
    raws = refs[22:24]
    sem_pieces, sem_feats, sem_out = refs[24:]
    c, x, y = at[0], at[1], at[2]
    side = y // 2
    scale = scalars[0]

    loads = [pltpu.make_async_copy(p, held.at[i], sem_pieces.at[i]) for i, p in enumerate(pieces)]
    for copy in loads:
        copy.start()

    def feat_load(i, source):
        return pltpu.make_async_copy(source, feats.at[pl.ds(i * BLOCK, BLOCK)], sem_feats.at[i])

    for copy in loads:
        copy.wait()
    for which, (own, other) in enumerate(((img_in, txt_in), (txt_in, img_in))):

        @pl.when(side == which)
        def _():
            feat_load(0, own).start()
            feat_load(1, other).start()

    def put(i, _):
        source, far, near = i // 16, i // 4 % 4, i % 4
        role = jnp.where(source == 0, c, 1 - c)
        px, py = position(role, x, y, near, far)
        start = role * D + (py % 2 * 4 + px) * BAND
        for half in range(2):

            @pl.when(py // 2 == half)
            def _():
                for q in range(4):
                    cols = slice(half * WIDE + q * 128, half * WIDE + q * 128 + 128)
                    heads[aligned(start, BAND, BAND), cols] = held[
                        source * 4 + far, near, q * BAND : (q + 1) * BAND, :
                    ]
                tail = held[source * 4 + far, near, 4 * BAND :, :]
                cols = slice(2 * WIDE + half * 64, 2 * WIDE + half * 64 + 64)
                heads[aligned(start, UPPER, 16), cols] = tail[:, :64]
                heads[aligned(start + UPPER, BAND - UPPER, 16), cols] = tail[: BAND - UPPER, 64:]

        return 0

    lax.fori_loop(0, 32, put, 0)
    for i in range(2):
        feat_load(i, img_in).wait()

    own_base = pl.multiple_of(side * D, D)
    other_base = pl.multiple_of((1 - side) * D, D)

    def project(i, raw, base):
        rows = aligned(i * CHUNK, CHUNK, CHUNK)
        for start in range(0, D, 256):
            width = min(256, D - start)
            cols = slice(start, start + width)
            raw[:, cols] = jnp.dot(
                feats[rows, :], heads[pl.ds(base, D), cols], preferred_element_type=f32
            )

    def finish(i, raw, own=False):
        rows = aligned(i * CHUNK, CHUNK, CHUNK)
        proj = raw[...]
        square = jnp.sum(proj * proj, axis=1, keepdims=True)
        inverse = 1.0 / jnp.sqrt(square + epsilon)
        unit = proj * inverse
        lows[rows, :] = unit.astype(bf16)
        if own:
            units[rows, :] = unit
            scales[rows, :] = jnp.broadcast_to(inverse * scale, (CHUNK, 128))
            flipped[:, rows] = feats[rows, :].T

    other_heads = heads.at[pl.ds(other_base, D)]
    stores = [
        pltpu.make_async_copy(ref, out, sem_out.at[i])
        for i, (ref, out) in enumerate(zip((other_heads, units, lows, flipped, scales), outs))
    ]
    stores[0].start()
    project(0, raws[0], own_base)
    finish(0, raws[0], own=True)
    project(1, raws[1], own_base)
    finish(1, raws[1], own=True)
    for i in (1, 3, 4):
        stores[i].start()
    project(2, raws[0], other_base)
    finish(2, raws[0])
    project(3, raws[1], other_base)
    finish(3, raws[1])
    stores[2].start()
    for copy in stores:
        copy.wait()


def second_kernel(at, scalars, *refs):
    heads_in, units_in, lows_in, flipped_in, scales_in = refs[:5]
    near_in, far_in = refs[5:7]
    halves_in = refs[7:11]
    kept, sent = refs[11:13]
    feats, flipped, heads, units, lows, scales, weights, rounded, staged = refs[13:22]
    raws, scores = refs[22:24], refs[24:26]
    sem_kept, sem_last, sem_halves, sem_out = refs[26:]
    c, x, y, z = at[0], at[1], at[2], at[3]
    side = y // 2
    scale, bias = scalars[0], scalars[1]
    half_loads = [
        pltpu.make_async_copy(source, feats.at[pl.ds(i * CHUNK, CHUNK)], sem_halves.at[i])
        for i, source in enumerate(halves_in)
    ]

    def last_load(source):
        return pltpu.make_async_copy(source, feats.at[pl.ds(2 * BLOCK, BLOCK)], sem_last.at[0])

    kept_loads = [
        pltpu.make_async_copy(source, to, sem_kept.at[i])
        for i, (source, to) in enumerate(
            (
                (heads_in, heads),
                (units_in, units),
                (lows_in, lows.at[pl.ds(0, 2 * BLOCK)]),
                (flipped_in, flipped),
                (scales_in, scales),
            )
        )
    ]
    kept_loads[0].start()
    for copy in half_loads:
        copy.start()
    for which, source in enumerate((far_in, near_in)):

        @pl.when((c + side) % 2 == which)
        def _():
            last_load(source).start()

    kept_loads[0].wait()
    for copy in half_loads:
        copy.wait()
    for copy in kept_loads[1:]:
        copy.start()

    def project(i, raw):
        rows = aligned(i * CHUNK, CHUNK, CHUNK)
        for start in range(0, D, 256):
            width = min(256, D - start)
            cols = slice(start, start + width)
            raw[:, cols] = jnp.dot(feats[rows, :], heads[:, cols], preferred_element_type=f32)

    def finish(i, raw):
        rows = aligned(2 * BLOCK + i * CHUNK, CHUNK, CHUNK)
        proj = raw[...]
        square = jnp.sum(proj * proj, axis=1, keepdims=True)
        lows[rows, :] = (proj * (1.0 / jnp.sqrt(square + epsilon))).astype(bf16)

    project(0, raws[0])

    def two(j, _):
        finish(2 * j, raws[0])
        project(2 * j + 1, raws[1])
        finish(2 * j + 1, raws[1])
        project(2 * j + 2, raws[0])
        return 0

    lax.fori_loop(0, 1, two, 0)
    last_load(far_in).wait()
    lax.fori_loop(1, 2, two, 0)
    finish(4, raws[0])
    project(5, raws[1])
    finish(5, raws[1])
    for copy in kept_loads[1:]:
        copy.wait()

    def score(t, to):
        rows = aligned(BLOCK + t * CHUNK, CHUNK, CHUNK)
        to[...] = rdot(lows[:BLOCK, :], lows[rows, :])

    def weigh(t, came, own=False):
        logits = scale * came[...] + bias
        half = 0.5
        if own:
            r = lax.broadcasted_iota(jnp.int32, logits.shape, 0)
            k = lax.broadcasted_iota(jnp.int32, logits.shape, 1) + t * CHUNK
            half = jnp.where(r == k, -0.5, 0.5)
        share = 0.5 * jnp.tanh(half * logits) + 0.5
        share = 2.0 * half * share if own else share
        weights[:, aligned(t * CHUNK, CHUNK, CHUNK)] = share.astype(bf16)

    score(0, scores[0])
    weigh(0, scores[0], own=True)
    score(1, scores[1])
    weigh(1, scores[1], own=True)
    score(2, scores[0])

    def pair(j, _):
        weigh(2 * j + 2, scores[0])
        score(2 * j + 3, scores[1])
        weigh(2 * j + 3, scores[1])
        score(2 * j + 4, scores[0])
        return 0

    lax.fori_loop(0, 2, pair, 0)
    weigh(6, scores[0])
    score(7, scores[1])
    weigh(7, scores[1])

    def gradient(i, _):
        rows = aligned(i * 192, 192, 192)
        grad = jnp.dot(weights[rows, :], lows[BLOCK:, :], preferred_element_type=f32)
        rounded[rows, :] = before(units, scales, rows, grad)
        return 0

    lax.fori_loop(0, BLOCK // 192, gradient, 0)

    for half in range(2):
        left = slice(half * D // 2, (half + 1) * D // 2)
        for start in range(0, D, 256):
            width = min(256, D - start)
            total = jnp.dot(
                flipped[left, :], rounded[:, start : start + width], preferred_element_type=f32
            )
            for px in range(4):
                for pz in range(4):
                    dx, dz = (px + 4 - x) % 4, (pz + 4 - z) % 4
                    near, far = (dx, dz) if half == 0 else (dz, dx)
                    row = (px * 4 + pz) * SHARE
                    for q in range(width // 128):
                        to = (start // 128 + q) * SHARE
                        staged[half, near, far, to : to + SHARE, :] = total[
                            row : row + SHARE, q * 128 : (q + 1) * 128
                        ]
        for which, out in enumerate((kept, sent)):

            @pl.when(c == (half if which == 0 else 1 - half))
            def _():
                pltpu.make_async_copy(staged.at[half], out, sem_out.at[half]).start()

    for half in range(2):
        pltpu.make_async_copy(staged.at[half], kept, sem_out.at[half]).wait()


def scratch(shape, kind=bf16):
    return pltpu.VMEM(shape, kind)


def first(at, scalars, pieces, feats):
    anywhere = pl.BlockSpec(memory_space=pl.ANY)
    smem = pl.BlockSpec(memory_space=pltpu.SMEM)
    shape = jax.ShapeDtypeStruct
    return pl.pallas_call(
        first_kernel,
        out_shape=[
            shape((D, D), bf16),
            shape((BLOCK, D), f32),
            shape((2 * BLOCK, D), bf16),
            shape((D, BLOCK), bf16),
            shape((BLOCK, 128), f32),
        ],
        in_specs=[smem, smem] + [anywhere] * 10,
        out_specs=[anywhere] * 5,
        scratch_shapes=[
            scratch((8, RING, PIECE, 128)),
            scratch((2 * BLOCK, D)),
            scratch((D, BLOCK)),
            scratch((2 * D, D)),
            scratch((BLOCK, D), f32),
            scratch((2 * BLOCK, D)),
            scratch((BLOCK, 128), f32),
            scratch((CHUNK, D), f32),
            scratch((CHUNK, D), f32),
            pltpu.SemaphoreType.DMA((8,)),
            pltpu.SemaphoreType.DMA((2,)),
            pltpu.SemaphoreType.DMA((5,)),
        ],
        compiler_params=pltpu.CompilerParams(vmem_limit_bytes=60 * 2**20),
        cost_estimate=pl.CostEstimate(
            flops=4_100_000_000, bytes_accessed=20_000_000, transcendentals=0
        ),
        name="first",
    )(at, scalars, *pieces, *feats)


def second(at, scalars, held, feats):
    anywhere = pl.BlockSpec(memory_space=pl.ANY)
    smem = pl.BlockSpec(memory_space=pltpu.SMEM)
    result = jax.ShapeDtypeStruct((RING, RING, PART, 128), f32)
    return pl.pallas_call(
        second_kernel,
        out_shape=[result, result],
        in_specs=[smem, smem] + [anywhere] * 11,
        out_specs=[anywhere] * 2,
        scratch_shapes=[
            scratch((3 * BLOCK, D)),
            scratch((D, BLOCK)),
            scratch((D, D)),
            scratch((BLOCK, D), f32),
            scratch((ROWS, D)),
            scratch((BLOCK, 128), f32),
            scratch((BLOCK, OTHERS)),
            scratch((BLOCK, D)),
            scratch((2, RING, RING, PART, 128), f32),
            scratch((CHUNK, D), f32),
            scratch((CHUNK, D), f32),
            scratch((BLOCK, CHUNK), f32),
            scratch((BLOCK, CHUNK), f32),
            pltpu.SemaphoreType.DMA((5,)),
            pltpu.SemaphoreType.DMA((1,)),
            pltpu.SemaphoreType.DMA((4,)),
            pltpu.SemaphoreType.DMA((2,)),
        ],
        compiler_params=pltpu.CompilerParams(vmem_limit_bytes=60 * 2**20),
        cost_estimate=pl.CostEstimate(
            flops=19_000_000_000, bytes_accessed=22_000_000, transcendentals=2_400_000
        ),
        name="second",
    )(at, scalars, *held, *feats)


def piece_kernel(at, *refs):
    parts, out, whole = refs[:4], refs[4], refs[5]
    z = at[3]
    for d in range(RING):
        for pz in range(RING):

            @pl.when((z + d) % RING == pz)
            def _():
                whole[pz * SHARE : (pz + 1) * SHARE, :] = parts[d][...].astype(f32)

    for q in range(4):
        out[q * BAND : (q + 1) * BAND, :] = whole[:, q * 128 : (q + 1) * 128].astype(bf16)
    lower = jnp.concatenate(
        [whole[UPPER:, WIDE:], jnp.zeros((2 * UPPER - BAND, 64), f32)], axis=0
    )
    out[4 * BAND :, :] = joined(whole[:UPPER, WIDE:], lower).astype(bf16)


def make_piece(at, parts):
    vmem = pl.BlockSpec(memory_space=pltpu.VMEM)
    return pl.pallas_call(
        piece_kernel,
        out_shape=jax.ShapeDtypeStruct((PIECE, 128), bf16),
        in_specs=[pl.BlockSpec(memory_space=pltpu.SMEM)] + [vmem] * 4,
        out_specs=vmem,
        scratch_shapes=[pltpu.VMEM((BAND, 576), f32)],
        compiler_params=pltpu.CompilerParams(vmem_limit_bytes=8 * 2**20),
        name="make_piece",
    )(at, *parts)


def share_kernel(at, *refs):
    parts, outs = refs[:4], refs[4:]
    c, y = at[0], at[2]
    yl, yh = y % 2, y // 2
    total = parts[0][...] + parts[1][...] + parts[2][...] + parts[3][...]
    for to_core in range(2):
        rows = [
            total[q * SHARE + to_core * 18 : q * SHARE + to_core * 18 + 18, :] for q in range(9)
        ]
        for to_half in range(2):
            tail = rows[8][:, to_half * 64 : to_half * 64 + 64]
            value = jnp.concatenate(rows[4 * to_half : 4 * to_half + 4] + [tail], axis=1)
            for a in range(2):
                for b in range(2):

                    @pl.when((yl == to_core ^ a) & (yh == to_half ^ b))
                    def _():
                        outs[a * 2 + b][...] = value


def make_shares(at, parts):
    vmem = pl.BlockSpec(memory_space=pltpu.VMEM)
    return pl.pallas_call(
        share_kernel,
        out_shape=[jax.ShapeDtypeStruct((18, 576), f32)] * 4,
        in_specs=[pl.BlockSpec(memory_space=pltpu.SMEM)] + [vmem] * 4,
        out_specs=[vmem] * 4,
        compiler_params=pltpu.CompilerParams(vmem_limit_bytes=8 * 2**20),
        name="make_shares",
    )(at, *parts)


def per_device(img_feat, txt_feat, img_head, txt_head, logit_scale, logit_bias):
    yl, x, z, c, yh = (lax.axis_index(a) for a in AXES)
    y = yh * 2 + yl
    at = jnp.stack([c, x, y, z]).astype(jnp.int32)

    is_first = c == 0
    mine = jnp.where(is_first, img_head, txt_head)
    come = moved(jnp.where(is_first, txt_head, img_head), partner)
    rows36 = jnp.where(
        is_first, jnp.concatenate([mine, come], 0), jnp.concatenate([come, mine], 0)
    )
    parts = [rows36] + [moved(rows36, along_z(-d)) for d in range(1, RING)]
    piece = make_piece(at, parts)

    other_feat = jnp.where(yh == 0, txt_feat, img_feat)
    upper, lower = other_feat[:CHUNK], other_feat[CHUNK:]
    piece, other_feat = lax.optimization_barrier((piece, other_feat))
    next_leg = moved(other_feat, mirrored(first_leg))

    near = [piece] + [moved(piece, by_core(along_x(-d), along_y(-d))) for d in range(1, RING)]
    near = jnp.stack(near)
    near, upper = lax.optimization_barrier((near, upper))
    far = [near] + [moved(near, by_core(along_y(-d), along_x(-d))) for d in range(1, RING)]
    upper = moved(upper, mirrored(two_on))
    leg, lower, _ = lax.optimization_barrier((next_leg, lower, far))
    lower = moved(lower, mirrored(two_on))
    last_leg = moved(leg, mirrored(second_leg))
    other = [moved(a, partner) for a in far]
    scalars = jnp.concatenate([logit_scale, logit_bias])
    held = first(at, scalars, far + other, [img_feat, txt_feat])
    upper, lower, held = lax.optimization_barrier((upper, lower, held))
    halves = [upper, lower, moved(upper, partner), moved(lower, partner)]
    kept, sent = second(at, scalars, held, [next_leg, last_leg] + halves)

    come = moved(sent, partner)
    total = kept[0] + come[0]
    for d in range(1, RING):
        share = (kept[d] + come[d]).astype(bf16)
        total = total + moved(share, by_core(along_x(d), along_z(d))).astype(f32)
    parts = [total[0]]
    for d in range(1, RING):
        parts.append(moved(total[d], by_core(along_z(d), along_x(d))))
    shares = make_shares(at, parts)
    results = []
    for b in range(2):
        results.append(moved(shares[b], to_owner(0, b)) + moved(shares[2 + b], to_owner(1, b)))
    return (
        jnp.where(yh == 0, results[0], results[1]),
        jnp.where(yh == 0, results[1], results[0]),
    )


def solution(mesh):
    split = Mesh(mesh.devices.reshape(SIZES), AXES)
    rows, cols = P(DP, None), P(DP, "yh")
    return jax.shard_map(
        per_device,
        mesh=split,
        in_specs=(rows, rows, cols, cols, P(), P()),
        out_specs=(cols, cols),
        check_vma=False,
    )
```
